128 devices in a mesh: dp: 4 (over x), block: 32 (over z, y, core).
Axes of the slice: x: 4, y: 4, z: 4, core: 2. Of those that a mesh axis runs over, the one named last changes fastest.
Arguments:
- grad_partial: float32 [4, 4, 32, 512, 512], P('dp', None, None, 'block'), may hold values from -6 to 6
- owner_table: int32 [4, 32], replicated, may hold values from 0 to 31, as said below
- left_factor: float32 [4, 32, 2, 512, 512], P('dp', 'block'), as said below
- right_factor: float32 [4, 32, 2, 512, 512], P('dp', 'block'), as said below
Outputs:
- update: bfloat16 [4, 32, 512, 512], P('dp', None, 'block')
- left_out: float32 [4, 32, 2, 512, 512], P('dp', 'block')
- right_out: float32 [4, 32, 2, 512, 512], P('dp', 'block')
The draws below stay inside these ranges and needn't reach their ends.
Inputs may be any that keep to these rules, and one draw needn't show every extreme that they name: owner_table[d, j] is the owner of block (d, j); within each row d no owner appears more than 2 times, and some owner appears exactly 2 times. `left_factor`: each slot holds a symmetric positive definite matrix. `right_factor`: each slot holds a symmetric positive definite matrix.
All inputs are finite; a program needn't handle non-finite values.
Results may differ from the reference program's by a relative error of at most 0.0072.
Values may be sent and summed in bfloat16 or wider, within the bound.
A program may use at most 128 MiB of HBM per device.

```python
import jax
import jax.numpy as jnp
from jax import lax

P_SIZE = 512
MOST = 2
ITERS = 3
POWER = 8
N_DP = 4
N_BLOCK = 32


def owner_row(row_key):
    first_key, second_key, third_key = jax.random.split(row_key, 3)
    shuffled = jax.random.permutation(first_key, N_BLOCK)
    paired = jax.random.randint(second_key, (), 1, N_BLOCK // 2 + 1)
    position = jnp.arange(N_BLOCK)
    later = jnp.clip(position - paired, 0, N_BLOCK - 1)
    chosen = jnp.where(position < 2 * paired, shuffled[position // 2], shuffled[later])
    return chosen[jax.random.permutation(third_key, N_BLOCK)].astype(jnp.int32)


def draw_owner_table(key, part):
    row_keys = jax.random.split(jax.random.fold_in(key, 11), N_DP)
    return jax.vmap(owner_row)(row_keys)


def factor_draw(key):
    first_key = jax.random.fold_in(key, 0)
    matrix = jax.random.normal(first_key, (N_DP, N_BLOCK, MOST, P_SIZE, P_SIZE), jnp.float32)
    return jnp.einsum('abcij,abckj->abcik', matrix, matrix) / P_SIZE


def draw_left_factor(key, part):
    return factor_draw(jax.random.fold_in(key, 21))


def draw_right_factor(key, part):
    return factor_draw(jax.random.fold_in(key, 31))


def shard_levels(own_key, shape, shards, smallest, largest):
    factor_of, own = 1.0, jax.random.fold_in(own_key, 6)
    for dim, shards_of in shards:
        heights = jnp.exp(jax.random.uniform(jax.random.fold_in(own, dim), (shards_of,), jnp.float32, smallest / len(shards), largest / len(shards)))
        factor_of = factor_of * jnp.repeat(heights, shape[dim] // shards_of).reshape([-1 if axis == dim else 1 for axis in range(len(shape))])
    return factor_of


def bell_draw(rng, dims, spread, reach, pieces=(), kind=jnp.bfloat16):
    level = shard_levels(rng, dims, pieces, -0.22, 0.18) if pieces else 1.0
    drawn = jax.random.normal(rng, dims, jnp.float32) * spread * level
    return jnp.minimum(jnp.maximum(drawn, -reach), reach).astype(kind)


def setup_inputs(seed: int = 0) -> dict:
    key_list = jax.random.split(jax.random.key(seed), 5)
    grad_partial = bell_draw(key_list[0], (N_DP, N_DP, N_BLOCK, P_SIZE, P_SIZE), 1.0, 6.0, ((0, 4), (3, 32)), jnp.float32)
    owner_table = draw_owner_table(jax.random.fold_in(key_list[4], 71), 0)
    left_factor = draw_left_factor(jax.random.fold_in(key_list[4], 71), 0)
    right_factor = draw_right_factor(jax.random.fold_in(key_list[4], 71), 0)
    return dict(grad_partial=grad_partial, owner_table=owner_table, left_factor=left_factor, right_factor=right_factor)


decay_rate = 0.9
damping = 0.1
epsilon = 1e-06

def inverse_root(factor):
    size = factor.shape[0]
    identity = jnp.eye(size, dtype=jnp.float32)
    shifted = factor + damping * identity
    vector = jnp.ones((size,), jnp.float32) / jnp.sqrt(jnp.float32(size))
    length = jnp.float32(1.0)
    for iteration in range(POWER):
        product = jnp.dot(shifted, vector, precision=lax.Precision.HIGHEST)
        length = jnp.sqrt(jnp.sum(product * product))
        vector = product / length
    ceiling = 1.25 * length
    scaled = shifted / ceiling
    inverse = identity * ceiling ** (-0.25)
    for iteration in range(ITERS):
        step_matrix = (5.0 * identity - scaled) / 4.0
        inverse = jnp.dot(inverse, step_matrix, precision=lax.Precision.HIGHEST)
        square = jnp.dot(step_matrix, step_matrix, precision=lax.Precision.HIGHEST)
        fourth = jnp.dot(square, square, precision=lax.Precision.HIGHEST)
        scaled = jnp.dot(fourth, scaled, precision=lax.Precision.HIGHEST)
    return inverse

def precondition(gradient, left_state, right_state):
    size = gradient.shape[0]
    left_term = jnp.dot(gradient, gradient.T, preferred_element_type=jnp.float32) / size
    right_term = jnp.dot(gradient.T, gradient, preferred_element_type=jnp.float32) / size
    new_left = decay_rate * left_state + (1.0 - decay_rate) * left_term
    new_right = decay_rate * right_state + (1.0 - decay_rate) * right_term
    left_root = inverse_root(new_left).astype(jnp.bfloat16)
    right_root = inverse_root(new_right).astype(jnp.bfloat16)
    half = jnp.dot(left_root, gradient, preferred_element_type=jnp.float32).astype(jnp.bfloat16)
    shaped = jnp.dot(half, right_root, preferred_element_type=jnp.float32)
    gradient_wide = gradient.astype(jnp.float32)
    graft_scale = jnp.sqrt(jnp.mean(gradient_wide * gradient_wide)) / jnp.sqrt(jnp.mean(shaped * shaped) + epsilon)
    return ((shaped * graft_scale).astype(jnp.bfloat16), new_left, new_right)

def reference(grad_partial, owner_table, left_factor, right_factor):
    summed = lax.optimization_barrier(jnp.sum(grad_partial, axis=0))
    gradient = summed.astype(jnp.bfloat16).reshape(N_DP * N_BLOCK, P_SIZE, P_SIZE)
    order = jnp.arange(N_BLOCK, dtype=jnp.int32)
    earlier = order[:, None] < order[None, :]
    matching = owner_table[:, :, None] == owner_table[:, None, :]
    slot_rank = lax.optimization_barrier(jnp.sum(jnp.logical_and(matching, earlier[None]), axis=1)).astype(jnp.int32)
    data_index = jnp.repeat(jnp.arange(N_DP, dtype=jnp.int32), N_BLOCK)
    owners = owner_table.reshape(-1).astype(jnp.int32)
    slot_index = slot_rank.reshape(-1)
    left_states = left_factor[data_index, owners, slot_index]
    right_states = right_factor[data_index, owners, slot_index]

    def per_block(block_items):
        return precondition(block_items[0], block_items[1], block_items[2])
    updates, new_lefts, new_rights = lax.map(per_block, (gradient, left_states, right_states))
    left_out = left_factor.at[data_index, owners, slot_index].set(new_lefts)
    right_out = right_factor.at[data_index, owners, slot_index].set(new_rights)
    updates = updates.reshape(N_DP, N_BLOCK, P_SIZE, P_SIZE)
    return (updates, left_out, right_out)
```

```python
import functools

import jax
import jax.numpy as jnp
from jax import lax
from jax.experimental import pallas as pl
from jax.experimental.pallas import tpu as pltpu
from jax.sharding import PartitionSpec as P

MOST = 2
POWER = 8
MESH = pl.DeviceIdType.MESH
F32 = jnp.float32
BF16 = jnp.bfloat16
MIB = 1 << 20

decay_rate = 0.9
damping = 0.1
epsilon = 1e-06

A1, A2, A3, A4, A5 = 625 / 256, -500 / 256, 150 / 256, -20 / 256, 1 / 256
R0 = 25 / 16
R1 = (-5 - 3125 / 256) / 16
R2 = 3125 / 256 / 16
R3 = -1250 / 256 / 16
R4 = 250 / 256 / 16
R5 = -25 / 256 / 16
R6 = 1 / 256 / 16


def dot(a, b):
    return jnp.dot(a, b, preferred_element_type=F32)


def gather_kernel(
    n_dp, count, lanes, table, grads, out, stage, raw, raw_in, cross, cross_in, both, both_in, summed,
    outgoing, load_sem, x_send, x_recv, o_send, o_recv,
):
    row, me = lax.axis_index("dp"), lax.axis_index("block")
    stripe = grads.shape[3]
    half = count // 2
    chunks = grads.shape[4] // lanes
    right, left, far = lax.rem(row + 1, n_dp), lax.rem(row + n_dp - 1, n_dp), lax.rem(row + 2, n_dp)

    barrier = pltpu.get_barrier_semaphore()
    for peer in (right, left):
        pl.semaphore_signal(barrier, inc=1, device_id=(peer, me), device_id_type=MESH)

    def greet(k, carry):
        pl.semaphore_signal(
            barrier, inc=1, device_id=(row, lax.rem(me + k, count)), device_id_type=MESH
        )
        return carry

    loads = []
    for n, d in enumerate((far, right, left, row)):
        load = pltpu.make_async_copy(grads.at[0, d], stage.at[n], load_sem.at[n])
        load.start()
        loads.append(load)
    lax.fori_loop(1, count, greet, 0)

    own_rows = pl.ds(pl.multiple_of(me * stripe, stripe), stripe)
    halves = (pl.ds(0, half), pl.ds(half, half))
    towards = (right, left)

    def cut(n, part, c):
        return stage[n, halves[part], :, pl.ds(c * lanes, lanes)]

    def x_copy(kind, way, c, src, dst):
        return pltpu.make_async_remote_copy(
            src_ref=src.at[way, c],
            dst_ref=dst.at[way, c],
            send_sem=x_send.at[kind, way, c],
            recv_sem=x_recv.at[kind, way, c],
            device_id=(towards[way], me),
            device_id_type=MESH,
        )

    loads[0].wait()
    for c in range(chunks):
        for way in range(2):
            raw[way, c] = cut(0, way, c).astype(BF16)
    loads[1].wait()
    loads[2].wait()
    for c in range(chunks):
        for way in range(2):
            cross[way, c] = cut(1 + way, 1 - way, c).astype(BF16)
    pl.semaphore_wait(barrier, count + 1)

    raws = [[x_copy(0, way, c, raw, raw_in) for way in range(2)] for c in range(chunks)]
    crosses = [[x_copy(1, way, c, cross, cross_in) for way in range(2)] for c in range(chunks)]
    boths = [[x_copy(2, way, c, both, both_in) for way in range(2)] for c in range(chunks)]

    def dispatch(c):
        columns = pl.ds(c * lanes, lanes)
        for way in range(2):
            crosses[c][way].wait_recv()
            boths[c][way].wait_recv()
        for part in range(2):
            total = cut(3, part, c) + both_in[part, c].astype(F32) + cross_in[1 - part, c].astype(F32)
            summed[c, halves[part]] = total.astype(BF16)

        def choose(o, carry):
            for s in range(MOST):
                outgoing[c, o, s] = summed[c, table[o * MOST + s]]
            return carry

        lax.fori_loop(0, count, choose, 0)

        def send(k, carry):
            o = lax.rem(me + k, count)
            pltpu.make_async_remote_copy(
                src_ref=outgoing.at[c, o],
                dst_ref=out.at[:, own_rows, columns],
                send_sem=o_send.at[c],
                recv_sem=o_recv.at[c],
                device_id=(row, o),
                device_id_type=MESH,
            ).start()
            return carry

        lax.fori_loop(1, count, send, 0)
        out[:, own_rows, columns] = outgoing[c, me]

    for way in range(2):
        raws[0][way].start()
    for c in range(chunks):
        if c + 1 < chunks:
            for way in range(2):
                raws[c + 1][way].start()
        for way in range(2):
            crosses[c][way].start()
        for way in range(2):
            raws[c][way].wait_recv()
            both[way, c] = (cut(1 + way, way, c) + raw_in[way, c].astype(F32)).astype(BF16)
            boths[c][way].start()
        if c == 0:
            loads[3].wait()
        if c > 0:
            dispatch(c - 1)
    dispatch(chunks - 1)

    for c in range(chunks):
        for way in range(2):
            raws[c][way].wait_send()
            crosses[c][way].wait_send()
            boths[c][way].wait_send()
    for c in range(chunks):
        arrived = outgoing.at[c, pl.ds(0, count - 1)]
        pltpu.make_async_copy(arrived, arrived, o_send.at[c]).wait()
        pltpu.make_async_copy(arrived, arrived, o_recv.at[c]).wait()


def gather_blocks(grads, table, n_dp, lanes):
    _, _, count, stripe, size = grads.shape
    chunks = size // lanes
    part = pltpu.VMEM((2, chunks, count // 2, stripe, lanes), BF16)
    return pl.pallas_call(
        functools.partial(gather_kernel, n_dp, count, lanes),
        name="gather_blocks",
        out_shape=jax.ShapeDtypeStruct((MOST, count * stripe, size), BF16),
        in_specs=[pl.BlockSpec(memory_space=pltpu.SMEM), pl.BlockSpec(memory_space=pl.ANY)],
        out_specs=pl.BlockSpec(memory_space=pltpu.VMEM),
        scratch_shapes=[
            pltpu.VMEM((4, count, stripe, size), F32),
            part, part, part, part, part, part,
            pltpu.VMEM((chunks, count, stripe, lanes), BF16),
            pltpu.VMEM((chunks, count, MOST, stripe, lanes), BF16),
            pltpu.SemaphoreType.DMA((4,)),
            pltpu.SemaphoreType.DMA((3, 2, chunks)),
            pltpu.SemaphoreType.DMA((3, 2, chunks)),
            pltpu.SemaphoreType.DMA((chunks,)),
            pltpu.SemaphoreType.DMA((chunks,)),
        ],
        compiler_params=pltpu.CompilerParams(
            collective_id=0, has_side_effects=True, vmem_limit_bytes=24 * MIB
        ),
    )(table, grads)


def diagonal(first, rows, size, value):
    down = lax.broadcasted_iota(jnp.int32, (rows, size), 0) + first
    across = lax.broadcasted_iota(jnp.int32, (rows, size), 1)
    return jnp.where(down == across, F32(value), F32(0))


def block_kernel(
    tall, active, blocks, left, right, left_out, right_out, result, flipped, factor, fresh, wide, wide2,
    m, u, v, w, load_sem, store_sem,
):
    size = blocks.shape[-1]
    chains = range(2 * MOST)
    tiles = [(i, pl.ds(i, tall)) for i in range(0, size, tall)]
    loads, stores = [], []
    for k in chains:
        slot, side = divmod(k, 2)
        load = pltpu.make_async_copy((left, right)[side].at[0, 0, slot], factor.at[k], load_sem.at[k])
        load.start()
        loads.append(load)
    for slot in range(MOST):
        flipped[slot] = blocks[slot].T

    def each(ks, step):
        for k in ks:
            for i, rows in tiles:
                step(k, i, rows)

    def gram(k, i, rows):
        slot, side = divmod(k, 2)
        first, second = (blocks, flipped) if side == 0 else (flipped, blocks)
        old = factor[k, rows, :]
        new = decay_rate * old + ((1.0 - decay_rate) / size) * dot(first[slot, rows, :], second[slot])
        fresh[k, rows, :] = jnp.where(active[slot] > 0, new, old)
        shifted = new + diagonal(i, tall, size, damping)
        wide[k, rows, :] = shifted
        m[k, rows, :] = shifted.astype(BF16)

    def roots(ks):
        for k in ks:
            loads[k].wait()
        each(ks, gram)
        for k in ks:
            slot, side = divmod(k, 2)
            store = pltpu.make_async_copy(
                fresh.at[k], (left_out, right_out)[side].at[0, 0, slot], store_sem.at[k]
            )
            store.start()
            stores.append(store)
        vector = {k: jnp.full((1, size), 1.0 / size**0.5, F32) for k in ks}
        length = {}
        for _ in range(POWER):
            for k in ks:
                high = vector[k].astype(BF16)
                low = (vector[k] - high.astype(F32)).astype(BF16)
                both = dot(jnp.concatenate([high, low], axis=0), m[k])
                product = both[0:1] + both[1:2]
                length[k] = jnp.sqrt(jnp.sum(product * product, axis=1, keepdims=True))
                vector[k] = product / length[k]
        ceiling = {k: 1.25 * length[k] for k in ks}
        inverse = {k: 1.0 / ceiling[k] for k in ks}
        scale = {k: lax.rsqrt(jnp.sqrt(ceiling[k])) for k in ks}

        def scaled(k, i, rows):
            value = wide[k, rows, :] * inverse[k]
            wide[k, rows, :] = value
            m[k, rows, :] = value.astype(BF16)

        def square(k, i, rows):
            product, value = dot(m[k, rows, :], m[k]), wide[k, rows, :]
            u[k, rows, :] = product.astype(BF16)
            wide[k, rows, :] = A1 * value + A2 * product
            v[k, rows, :] = (A4 * value + A5 * product).astype(BF16)

        def cube(k, i, rows):
            product = dot(m[k, rows, :], u[k])
            w[k, rows, :] = product.astype(BF16)
            wide[k, rows, :] += A3 * product

        def second(k, i, rows):
            value = wide[k, rows, :] + dot(w[k, rows, :], v[k])
            wide[k, rows, :] = value
            u[k, rows, :] = value.astype(BF16)

        def square_again(k, i, rows):
            product, value = dot(u[k, rows, :], u[k]), wide[k, rows, :]
            w[k, rows, :] = product.astype(BF16)
            wide[k, rows, :] = R1 * value + R2 * product
            wide2[k, rows, :] = R4 * value + R5 * product

        def cube_again(k, i, rows):
            product = dot(u[k, rows, :], w[k])
            wide[k, rows, :] += R3 * product
            v[k, rows, :] = (wide2[k, rows, :] + R6 * product).astype(BF16)
            wide2[k, rows, :] = product

        def tail(k, i, rows):
            value = wide[k, rows, :] + dot(wide2[k, rows, :].astype(BF16), v[k])
            value = value + diagonal(i, tall, size, R0)
            wide[k, rows, :] = value
            u[k, rows, :] = value.astype(BF16)

        def root(k, i, rows):
            value = 1.25 * wide[k, rows, :] - 0.25 * dot(m[k, rows, :], u[k])
            w[k, rows, :] = (value * scale[k]).astype(BF16)

        for step in (scaled, square, cube, second, square_again, cube_again, tail, root):
            each(ks, step)

    def shape_block(slot):
        one, two = 2 * slot, 2 * slot + 1
        for i, rows in tiles:
            u[one, rows, :] = dot(w[one, rows, :], blocks[slot]).astype(BF16)
        energy, power = jnp.zeros((1, size), F32), jnp.zeros((1, size), F32)
        for i, rows in tiles:
            shaped = dot(u[one, rows, :], w[two])
            wide[one, rows, :] = shaped
            original = blocks[slot, rows, :].astype(F32)
            energy += jnp.sum(shaped * shaped, axis=0, keepdims=True)
            power += jnp.sum(original * original, axis=0, keepdims=True)
        energy = jnp.sum(energy, axis=1, keepdims=True) / (size * size)
        power = jnp.sum(power, axis=1, keepdims=True) / (size * size)
        graft = jnp.sqrt(power) / jnp.sqrt(energy + epsilon)
        for i, rows in tiles:
            result[slot, rows, :] = (wide[one, rows, :] * graft).astype(BF16)

    roots(chains)
    for slot in range(MOST):
        shape_block(slot)
    for store in stores:
        store.wait()


def precondition(active, blocks, left, right, tall):
    size = blocks.shape[-1]
    wide = pltpu.VMEM((2 * MOST, size, size), F32)
    thin = pltpu.VMEM((2 * MOST, size, size), BF16)
    any_spec = pl.BlockSpec(memory_space=pl.ANY)
    vmem_spec = pl.BlockSpec(memory_space=pltpu.VMEM)
    return pl.pallas_call(
        functools.partial(block_kernel, tall),
        name="precondition",
        out_shape=(
            jax.ShapeDtypeStruct(left.shape, F32),
            jax.ShapeDtypeStruct(right.shape, F32),
            jax.ShapeDtypeStruct(blocks.shape, BF16),
        ),
        in_specs=[pl.BlockSpec(memory_space=pltpu.SMEM), vmem_spec, any_spec, any_spec],
        out_specs=(any_spec, any_spec, vmem_spec),
        scratch_shapes=[
            pltpu.VMEM((MOST, size, size), BF16),
            wide, wide, wide, wide, thin, thin, thin, thin,
            pltpu.SemaphoreType.DMA((2 * MOST,)),
            pltpu.SemaphoreType.DMA((2 * MOST,)),
        ],
        compiler_params=pltpu.CompilerParams(vmem_limit_bytes=48 * MIB),
    )(active, blocks, left, right)


def return_kernel(count, place, ready, update, back, send_sem, recv_sem):
    row, me = lax.axis_index("dp"), lax.axis_index("block")
    stripe = update.shape[1]
    barrier = pltpu.get_barrier_semaphore()

    def greet(k, carry):
        pl.semaphore_signal(
            barrier, inc=1, device_id=(row, lax.rem(me + k, count)), device_id_type=MESH
        )
        return carry

    lax.fori_loop(1, count, greet, 0)
    pl.semaphore_wait(barrier, count - 1)

    def send(k, carry):
        o = lax.rem(me + k, count)
        pltpu.make_async_remote_copy(
            src_ref=ready.at[:, pl.ds(pl.multiple_of(o * stripe, stripe), stripe), :],
            dst_ref=back.at[pl.ds(me * MOST, MOST)],
            send_sem=send_sem,
            recv_sem=recv_sem,
            device_id=(row, o),
            device_id_type=MESH,
        ).start()
        return carry

    lax.fori_loop(1, count, send, 0)
    back[pl.ds(me * MOST, MOST)] = ready[:, pl.ds(pl.multiple_of(me * stripe, stripe), stripe), :]
    arrived = back.at[pl.ds(0, MOST * (count - 1))]
    pltpu.make_async_copy(arrived, arrived, send_sem).wait()
    pltpu.make_async_copy(arrived, arrived, recv_sem).wait()

    def put(j, carry):
        update[j] = back[place[j]]
        return carry

    lax.fori_loop(0, count, put, 0)


def return_blocks(ready, place, count):
    _, rows, size = ready.shape
    vmem_spec = pl.BlockSpec(memory_space=pltpu.VMEM)
    stripe = rows // count
    return pl.pallas_call(
        functools.partial(return_kernel, count),
        name="return_blocks",
        out_shape=jax.ShapeDtypeStruct((count, stripe, size), BF16),
        in_specs=[pl.BlockSpec(memory_space=pltpu.SMEM), vmem_spec],
        out_specs=vmem_spec,
        scratch_shapes=[
            pltpu.VMEM((MOST * count, stripe, size), BF16),
            pltpu.SemaphoreType.DMA,
            pltpu.SemaphoreType.DMA,
        ],
        compiler_params=pltpu.CompilerParams(
            collective_id=1, has_side_effects=True, vmem_limit_bytes=16 * MIB
        ),
    )(place, ready)


def tables(owners):
    count = owners.shape[0]
    order = jnp.arange(count, dtype=jnp.int32)
    same = owners[:, None] == owners[None, :]
    rank = jnp.sum(same & (order[:, None] < order[None, :]), axis=0, dtype=jnp.int32)
    place = owners * MOST + rank
    slots = jnp.arange(MOST * count, dtype=jnp.int32)
    holds = place[None, :] == slots[:, None]
    block_of = jnp.sum(jnp.where(holds, order[None, :], 0), axis=1, dtype=jnp.int32)
    return place, block_of, jnp.any(holds, axis=1).astype(jnp.int32)


def local(n_dp, grad_partial, owner_table, left_factor, right_factor):
    row, me = lax.axis_index("dp"), lax.axis_index("block")
    owners = lax.dynamic_index_in_dim(owner_table, row, 0, keepdims=False)
    place, block_of, held = tables(owners)
    active = lax.dynamic_slice_in_dim(held, me * MOST, MOST, 0)
    count = owners.shape[0]
    blocks = gather_blocks(grad_partial, block_of, n_dp, 128)
    new_left, new_right, ready = precondition(active, blocks, left_factor, right_factor, 256)
    update = return_blocks(ready, place, count)
    return update[None], new_left, new_right


def solution(mesh):
    return jax.shard_map(
        functools.partial(local, mesh.shape["dp"]),
        mesh=mesh,
        in_specs=(
            P("dp", None, None, "block", None),
            P(),
            P("dp", "block", None, None, None),
            P("dp", "block", None, None, None),
        ),
        out_specs=(
            P("dp", None, "block", None),
            P("dp", "block", None, None, None),
            P("dp", "block", None, None, None),
        ),
        check_vma=False,
    )
```

```python
import functools

import jax
import jax.numpy as jnp
from jax import lax
from jax.experimental import pallas as pl
from jax.experimental.pallas import tpu as pltpu
from jax.sharding import PartitionSpec as P

MOST = 2
POWER = 8
SPREAD = 13
MESH = pl.DeviceIdType.MESH
F32 = jnp.float32
BF16 = jnp.bfloat16
MIB = 1 << 20

decay_rate = 0.9
damping = 0.1
epsilon = 1e-06

A1, A2, A3, A4, A5 = 625 / 256, -500 / 256, 150 / 256, -20 / 256, 1 / 256
R0 = 25 / 16
R1 = (-5 - 3125 / 256) / 16
R2 = 3125 / 256 / 16
R3 = -1250 / 256 / 16
R4 = 250 / 256 / 16
R5 = -25 / 256 / 16
R6 = 1 / 256 / 16


def dot(a, b):
    return jnp.dot(a, b, preferred_element_type=F32)


def tiles_of(size, tall, broad):
    return [(i, j, pl.ds(i, tall), pl.ds(j, broad)) for j in range(0, size, broad) for i in range(0, size, tall)]


def plus_diagonal(value, i, j, amount):
    tall, broad = value.shape
    if i + tall <= j or j + broad <= i:
        return value
    down = lax.broadcasted_iota(jnp.int32, (tall, broad), 0) + i
    across = lax.broadcasted_iota(jnp.int32, (tall, broad), 1) + j
    return value + jnp.where(down == across, amount, F32(0))


def whole_sum(value):
    return jnp.sum(jnp.sum(value, axis=0, keepdims=True), axis=1, keepdims=True)


def largest_diagonal(factor, k, size):
    best = None
    for i in range(0, size, 128):
        part = factor[k, pl.ds(i, 128), pl.ds(i, 128)]
        down = lax.broadcasted_iota(jnp.int32, (128, 128), 0)
        across = lax.broadcasted_iota(jnp.int32, (128, 128), 1)
        part = jnp.where(down == across, part, F32(0))
        best = part if best is None else jnp.maximum(best, part)
    return jnp.max(jnp.max(best, axis=0, keepdims=True), axis=1, keepdims=True)


def precondition(slot, active, shape, blocks, flipped, factor, fresh, b, u, v, w, m, wide, result):
    size = blocks.shape[-1]
    tiles = tiles_of(size, *shape)
    chains = (2 * slot, 2 * slot + 1)

    def each(step):
        for k in chains:
            for i, j, rows, columns in tiles:
                step(k, i, j, rows, columns)

    flipped[slot] = blocks[slot].T
    original = blocks[slot].astype(F32)
    energy_in = whole_sum(original * original)
    tops = {k: decay_rate * largest_diagonal(factor, k, size) + ((1.0 - decay_rate) / size) * energy_in + damping for k in chains}
    shrink = {k: 1.0 / tops[k] for k in chains}
    columns_sum = {k: {} for k in chains}
    keep = jnp.where(active, F32(decay_rate), F32(1.0))
    add = jnp.where(active, F32((1.0 - decay_rate) / size), F32(0.0))

    def gram(k, i, j, rows, columns):
        first, second = (blocks, flipped) if k % 2 == 0 else (flipped, blocks)
        old = factor[k, rows, columns]
        product = dot(first[slot, rows, :], second[slot, :, columns])
        new = keep * old + add * product
        fresh[k % 2][slot, rows, columns] = new
        value = plus_diagonal(new * shrink[k], i, j, damping * shrink[k])
        b[k, rows, columns] = value.astype(BF16)
        part = jnp.sum(value, axis=0, keepdims=True)
        columns_sum[k][j] = columns_sum[k][j] + part if j in columns_sum[k] else part

    def square(k, i, j, rows, columns):
        u[k, rows, columns] = dot(b[k, rows, :], b[k, :, columns]).astype(BF16)

    def cube(k, i, j, rows, columns):
        w[k, rows, columns] = dot(b[k, rows, :], u[k, :, columns]).astype(BF16)

    each(gram)
    each(square)
    each(cube)

    vector = {
        k: jnp.concatenate([columns_sum[k][j] for j in sorted(columns_sum[k])], axis=1) for k in chains
    }
    length = {}
    for turn, matrix in enumerate((w, w, b)):
        for k in chains:
            vector[k] = vector[k] * lax.rsqrt(jnp.sum(vector[k] * vector[k], axis=1, keepdims=True))
        for k in chains:
            high = vector[k].astype(BF16)
            low = (vector[k] - high.astype(F32)).astype(BF16)
            both = dot(jnp.concatenate([high, low], axis=0), matrix[k])
            vector[k] = both[0:1] + both[1:2]
    for k in chains:
        length[k] = jnp.sqrt(jnp.sum(vector[k] * vector[k], axis=1, keepdims=True))
    c1 = {k: 1.0 / (1.25 * length[k]) for k in chains}
    c2 = {k: c1[k] * c1[k] for k in chains}
    c3 = {k: c2[k] * c1[k] for k in chains}
    scale = {k: lax.rsqrt(jnp.sqrt((1.25 * length[k]) * tops[k])) for k in chains}

    def thin(scalar):
        return scalar.astype(BF16)

    def mixed(k, i, j, rows, columns):
        v[k, rows, columns] = (
            thin(A4 * c1[k]) * b[k, rows, columns] + thin(A5 * c2[k]) * u[k, rows, columns]
        )

    def second(k, i, j, rows, columns):
        value = c3[k] * dot(w[k, rows, :], v[k, :, columns])
        small = thin(A2 * c2[k]) * u[k, rows, columns] + thin(A3 * c3[k]) * w[k, rows, columns]
        value += (A1 * c1[k]) * b[k, rows, columns].astype(F32) + small.astype(F32)
        m[k, rows, columns] = value.astype(BF16)

    def square_again(k, i, j, rows, columns):
        u[k, rows, columns] = dot(m[k, rows, :], m[k, :, columns]).astype(BF16)

    def cube_again(k, i, j, rows, columns):
        product = dot(m[k, rows, :], u[k, :, columns]).astype(BF16)
        w[k, rows, columns] = product
        v[k, rows, columns] = (
            BF16(R4) * m[k, rows, columns] + BF16(R5) * u[k, rows, columns] + BF16(R6) * product
        )

    def tail(k, i, j, rows, columns):
        small = BF16(R2) * u[k, rows, columns] + BF16(R3) * w[k, rows, columns]
        value = dot(w[k, rows, :], v[k, :, columns]) + small.astype(F32)
        m[k, rows, columns] = (value + R1 * m[k, rows, columns].astype(F32)).astype(BF16)

    def root(k, i, j, rows, columns):
        value = (1.25 * scale[k]) * m[k, rows, columns].astype(F32)
        value -= (0.25 * R0 * scale[k] * c1[k]) * b[k, rows, columns].astype(F32)
        value -= (0.25 * scale[k] * c1[k]) * dot(b[k, rows, :], m[k, :, columns])
        v[k, rows, columns] = plus_diagonal(value, i, j, (1.25 * R0) * scale[k]).astype(BF16)

    for step in (mixed, second, square_again, cube_again, tail, root):
        each(step)

    one, two = chains
    for i, j, rows, columns in tiles:
        u[one, rows, columns] = dot(v[one, rows, :], blocks[slot, :, columns]).astype(BF16)
    energy = jnp.zeros((1, 1), F32)
    for i, j, rows, columns in tiles:
        shaped = dot(u[one, rows, :], v[two, :, columns])
        wide[rows, columns] = shaped
        energy += whole_sum(shaped * shaped)
    graft = jnp.sqrt(energy_in / (size * size)) / jnp.sqrt(energy / (size * size) + epsilon)
    for i, j, rows, columns in tiles:
        result[slot, rows, columns] = (wide[rows, columns] * graft).astype(BF16)


def step_kernel(
    n_dp, count, lanes, shape, owner_table, grads, left, right, update, left_new, right_new, owners_v, owners_s,
    place_v, place_s, block_v, block_s, stage, raw, raw_in, cross, cross_in, both, both_in, summed, outgoing,
    blocks, flipped, factor, b, u, v, w, m, wide, ready, back, load_sem, factor_sem, table_sem, x_send, x_recv,
    o_send, o_recv, r_send, r_recv,
):
    row, me = lax.axis_index("dp"), lax.axis_index("block")
    stripe = grads.shape[3]
    half = count // 2
    chunks = grads.shape[4] // lanes
    near, behind, far = lax.rem(row + 1, n_dp), lax.rem(row + n_dp - 1, n_dp), lax.rem(row + 2, n_dp)

    table_loads = [
        pltpu.make_async_copy(owner_table, owners_v, table_sem.at[0]),
        pltpu.make_async_copy(owner_table, owners_s, table_sem.at[1]),
    ]
    loads = [
        pltpu.make_async_copy(grads.at[0, d], stage.at[n], load_sem.at[n])
        for n, d in enumerate((far, near, behind, row))
    ]
    factor_loads = [
        pltpu.make_async_copy((left, right)[k % 2].at[0, 0, k // 2], factor.at[k], factor_sem.at[k])
        for k in range(2 * MOST)
    ]
    for load in (*loads, *table_loads):
        load.start()

    def partner(k):
        return lax.rem(me + SPREAD * k, count)

    barrier = pltpu.get_barrier_semaphore()
    for peer in (near, behind):
        pl.semaphore_signal(barrier, inc=1, device_id=(peer, me), device_id_type=MESH)

    def greet(k, carry):
        pl.semaphore_signal(barrier, inc=1, device_id=(row, partner(k)), device_id_type=MESH)
        return carry

    lax.fori_loop(1, count, greet, 0)

    own_rows = pl.ds(pl.multiple_of(me * stripe, stripe), stripe)
    halves = (pl.ds(0, half), pl.ds(half, half))
    towards = (near, behind)

    def cut(n, part, c):
        return stage[n, halves[part], :, pl.ds(c * lanes, lanes)]

    def x_copy(kind, way, c, src, dst):
        return pltpu.make_async_remote_copy(
            src_ref=src.at[way, c],
            dst_ref=dst.at[way, c],
            send_sem=x_send.at[kind, way, c],
            recv_sem=x_recv.at[kind, way, c],
            device_id=(towards[way], me),
            device_id_type=MESH,
        )

    raws = [[x_copy(0, way, c, raw, raw_in) for way in range(2)] for c in range(chunks)]
    crosses = [[x_copy(1, way, c, cross, cross_in) for way in range(2)] for c in range(chunks)]
    boths = [[x_copy(2, way, c, both, both_in) for way in range(2)] for c in range(chunks)]

    def dispatch(c):
        columns = pl.ds(c * lanes, lanes)
        for way in range(2):
            crosses[c][way].wait_recv()
            boths[c][way].wait_recv()
        for part in range(2):
            total = cut(3, part, c) + both_in[part, c].astype(F32) + cross_in[1 - part, c].astype(F32)
            summed[c, halves[part]] = total.astype(BF16)

        def send(k, carry):
            o = partner(k)
            for s in range(MOST):
                outgoing[c, o, s] = summed[c, block_s[0, o * MOST + s]]
            pltpu.make_async_remote_copy(
                src_ref=outgoing.at[c, o],
                dst_ref=blocks.at[:, own_rows, columns],
                send_sem=o_send.at[c],
                recv_sem=o_recv.at[c],
                device_id=(row, o),
                device_id_type=MESH,
            ).start()
            return carry

        lax.fori_loop(1, count, send, 0)
        for s in range(MOST):
            blocks[s, own_rows, columns] = summed[c, block_s[0, me * MOST + s]]

    loads[0].wait()
    for c in range(chunks):
        for way in range(2):
            raw[way, c] = cut(0, way, c).astype(BF16)
    loads[1].wait()
    loads[2].wait()
    for c in range(chunks):
        for way in range(2):
            cross[way, c] = cut(1 + way, 1 - way, c).astype(BF16)
    pl.semaphore_wait(barrier, count + 1)
    for way in range(2):
        raws[0][way].start()
    for way in range(2):
        crosses[0][way].start()
    for c in range(1, chunks):
        for way in range(2):
            raws[c][way].start()

    for load in table_loads:
        load.wait()
    owners = owners_v[pl.ds(row, 1), :]
    order = lax.broadcasted_iota(jnp.int32, owners.shape, 1)

    def count_same(j, ranks):
        same = (owners == owners_s[row, j]) & (order > j)
        return ranks + jnp.where(same, 1, 0)

    places = owners * MOST + lax.fori_loop(0, count, count_same, jnp.zeros_like(owners))
    place_v[...] = places
    place_copy = pltpu.make_async_copy(place_v, place_s, table_sem.at[2])
    place_copy.start()
    place_copy.wait()
    slots = lax.broadcasted_iota(jnp.int32, block_v.shape, 1)

    def fill(j, held):
        return jnp.where(slots == place_s[0, j], j, held)

    block_v[...] = lax.fori_loop(0, count, fill, jnp.zeros_like(slots))
    block_copy = pltpu.make_async_copy(block_v, block_s, table_sem.at[3])
    block_copy.start()
    block_copy.wait()
    loads[3].wait()
    for load in factor_loads:
        load.start()

    for c in range(chunks):
        if c > 0:
            for way in range(2):
                crosses[c][way].start()
        for way in range(2):
            raws[c][way].wait_recv()
            both[way, c] = (cut(1 + way, way, c) + raw_in[way, c].astype(F32)).astype(BF16)
            boths[c][way].start()
        if c > 0:
            dispatch(c - 1)
    dispatch(chunks - 1)
    for load in factor_loads:
        load.wait()
    for c in range(chunks):
        arrived = outgoing.at[c, pl.ds(0, count - 1)]
        pltpu.make_async_copy(arrived, arrived, o_recv.at[c]).wait()

    for slot in range(MOST):
        used = jnp.where(places == me * MOST + slot, F32(1), F32(0))
        active = jnp.max(used, axis=1, keepdims=True) > 0.5
        precondition(
            slot, active, shape, blocks, flipped, factor, (left_new, right_new), b, u, v, w, m, wide, ready
        )

        def give(k, carry):
            o = partner(k)
            pltpu.make_async_remote_copy(
                src_ref=ready.at[slot, pl.ds(pl.multiple_of(o * stripe, stripe), stripe)],
                dst_ref=back.at[me * MOST + slot],
                send_sem=r_send.at[slot],
                recv_sem=r_recv.at[slot],
                device_id=(row, o),
                device_id_type=MESH,
            ).start()
            return carry

        lax.fori_loop(1, count, give, 0)
        back[me * MOST + slot] = ready[slot, own_rows]

    for c in range(chunks):
        for way in range(2):
            raws[c][way].wait_send()
            crosses[c][way].wait_send()
            boths[c][way].wait_send()
        arrived = outgoing.at[c, pl.ds(0, count - 1)]
        pltpu.make_async_copy(arrived, arrived, o_send.at[c]).wait()
    for slot in range(MOST):
        arrived = back.at[pl.ds(0, count - 1)]
        pltpu.make_async_copy(arrived, arrived, r_recv.at[slot]).wait()
        pltpu.make_async_copy(arrived, arrived, r_send.at[slot]).wait()

    def put(j, carry):
        update[j] = back[place_s[0, j]]
        return carry

    lax.fori_loop(0, count, put, 0)


def whole_step(owner_table, grads, left, right, n_dp, lanes, shape):
    _, _, count, stripe, size = grads.shape
    chunks = size // lanes
    part = pltpu.VMEM((2, chunks, count // 2, stripe, lanes), BF16)
    thin = pltpu.VMEM((2 * MOST, size, size), BF16)
    pair = pltpu.VMEM((MOST, size, size), BF16)
    slots = -(-MOST * count // 128) * 128
    DMA = pltpu.SemaphoreType.DMA
    hbm, vmem = pl.BlockSpec(memory_space=pltpu.HBM), pl.BlockSpec(memory_space=pltpu.VMEM)
    return pl.pallas_call(
        functools.partial(step_kernel, n_dp, count, lanes, shape),
        name="shampoo_step",
        out_shape=(
            jax.ShapeDtypeStruct((count, stripe, size), BF16),
            jax.ShapeDtypeStruct((MOST, size, size), F32),
            jax.ShapeDtypeStruct((MOST, size, size), F32),
        ),
        in_specs=[hbm, hbm, hbm, hbm],
        out_specs=(vmem, vmem, vmem),
        scratch_shapes=[
            pltpu.VMEM((n_dp, count), jnp.int32),
            pltpu.SMEM((n_dp, count), jnp.int32),
            pltpu.VMEM((1, count), jnp.int32),
            pltpu.SMEM((1, count), jnp.int32),
            pltpu.VMEM((1, slots), jnp.int32),
            pltpu.SMEM((1, slots), jnp.int32),
            pltpu.VMEM((4, count, stripe, size), F32),
            part, part, part, part, part, part,
            pltpu.VMEM((chunks, count, stripe, lanes), BF16),
            pltpu.VMEM((chunks, count, MOST, stripe, lanes), BF16),
            pair, pair,
            pltpu.VMEM((2 * MOST, size, size), F32),
            thin, thin, thin, thin, thin,
            pltpu.VMEM((size, size), F32),
            pair,
            pltpu.VMEM((MOST * count, stripe, size), BF16),
            DMA((4,)), DMA((2 * MOST,)), DMA((4,)), DMA((3, 2, chunks)), DMA((3, 2, chunks)),
            DMA((chunks,)), DMA((chunks,)), DMA((MOST,)), DMA((MOST,)),
        ],
        compiler_params=pltpu.CompilerParams(
            collective_id=0, has_side_effects=True, vmem_limit_bytes=48 * MIB
        ),
    )(owner_table, grads, left, right)


def store_kernel(*refs):
    sources, targets, sems = refs[:3], refs[3:6], refs[6]
    copies = [pltpu.make_async_copy(s, t, sems.at[n]) for n, (s, t) in enumerate(zip(sources, targets))]
    for copy in copies:
        copy.start()
    for copy in copies:
        copy.wait()


def store(*values):
    return pl.pallas_call(
        store_kernel,
        name="store",
        out_shape=tuple(jax.ShapeDtypeStruct(x.shape, x.dtype) for x in values),
        in_specs=[pl.BlockSpec(memory_space=pltpu.VMEM)] * 3,
        out_specs=tuple([pl.BlockSpec(memory_space=pltpu.HBM)] * 3),
        scratch_shapes=[pltpu.SemaphoreType.DMA((3,))],
        compiler_params=pltpu.CompilerParams(vmem_limit_bytes=8 * MIB),
    )(*values)


def local(n_dp, grad_partial, owner_table, left_factor, right_factor):
    values = whole_step(owner_table, grad_partial, left_factor, right_factor, n_dp, 128, (512, 256))
    update, new_left, new_right = store(*values)
    return update[None], new_left[None, None], new_right[None, None]


def solution(mesh):
    return jax.shard_map(
        functools.partial(local, mesh.shape["dp"]),
        mesh=mesh,
        in_specs=(
            P("dp", None, None, "block", None),
            P(),
            P("dp", "block", None, None, None),
            P("dp", "block", None, None, None),
        ),
        out_specs=(
            P("dp", None, "block", None),
            P("dp", "block", None, None, None),
            P("dp", "block", None, None, None),
        ),
        check_vma=False,
    )
```

```python
import functools

import jax
import jax.numpy as jnp
from jax import lax
from jax.experimental import pallas as pl
from jax.experimental.pallas import tpu as pltpu
from jax.sharding import PartitionSpec as P

MOST = 2
POWER = 8
SIDE = 4


def distance(hop):
    return sum(min(steps, SIDE - steps) for steps in hop[:2])


HOPS = sorted(
    ((z, y, core) for z in range(SIDE) for y in range(SIDE) for core in range(2) if (z, y, core) != (0, 0, 0)),
    key=lambda hop: (-distance(hop), (hop[0] + hop[1]) % 2, hop),
)
MESH = pl.DeviceIdType.MESH
F32 = jnp.float32
BF16 = jnp.bfloat16
MIB = 1 << 20
PIECES = 4

decay_rate = 0.9
damping = 0.1
epsilon = 1e-06

A1, A2, A3, A4, A5 = 625 / 256, -500 / 256, 150 / 256, -20 / 256, 1 / 256
R0 = 25 / 16
R1 = (-5 - 3125 / 256) / 16
R2 = 3125 / 256 / 16
R3 = -1250 / 256 / 16
R4 = 250 / 256 / 16
R5 = -25 / 256 / 16
R6 = 1 / 256 / 16


def dot(a, b):
    return jnp.dot(a, b, preferred_element_type=F32)


def plus_diagonal(value, i, j, amount):
    tall, broad = value.shape
    if i + tall <= j or j + broad <= i:
        return value
    down = lax.broadcasted_iota(jnp.int32, (tall, broad), 0) + i
    across = lax.broadcasted_iota(jnp.int32, (tall, broad), 1) + j
    return value + jnp.where(down == across, amount, F32(0))


def whole_sum(value):
    return jnp.sum(jnp.sum(value, axis=0, keepdims=True), axis=1, keepdims=True)


def largest_diagonal(factor, k, size):
    best = None
    for i in range(0, size, 128):
        part = factor[k, pl.ds(i, 128), pl.ds(i, 128)]
        down = lax.broadcasted_iota(jnp.int32, (128, 128), 0)
        across = lax.broadcasted_iota(jnp.int32, (128, 128), 1)
        part = jnp.where(down == across, part, F32(0))
        best = part if best is None else jnp.maximum(best, part)
    return jnp.max(jnp.max(best, axis=0, keepdims=True), axis=1, keepdims=True)


def absorb(slot, c, lanes, blocks, flipped, sums, last):
    columns = pl.ds(c * lanes, lanes)
    piece = blocks[slot, :, columns]
    flipped[slot, columns, :] = piece.T
    wide = piece.astype(F32)
    energy = jnp.sum(wide * wide, axis=0, keepdims=True)
    one, two = 2 * slot, 2 * slot + 1
    if not last:
        product = dot(piece, flipped[slot, columns, :])
        sums[one] = product if c == 0 else sums[one] + product
    seen = (c + 1) * lanes
    product = dot(flipped[slot, pl.ds(0, seen), :], piece)
    sums[two, pl.ds(0, seen), columns] = product
    if c > 0:
        sums[two, columns, pl.ds(0, c * lanes)] = product[: c * lanes].T
    return energy


def precondition(slot, active, tile, lanes, energy_in, tops, blocks, flipped, sums, factor, fresh, b, u, v, w, m, wide, result):
    size = blocks.shape[-1]
    chains = (2 * slot, 2 * slot + 1)
    offsets = range(0, size, tile)
    energy_in = jnp.sum(energy_in, axis=1, keepdims=True)
    grown = ((1.0 - decay_rate) / size) * energy_in + damping
    tops = {k: tops[k] + grown for k in chains}
    shrink = {k: 1.0 / tops[k] for k in chains}
    columns_sum = {k: {} for k in chains}
    keep = jnp.where(active, F32(decay_rate), F32(1.0))
    add = jnp.where(active, F32((1.0 - decay_rate) / size), F32(0.0))

    def gram(k, i, j, rows, columns):
        product = sums[k, rows, columns]
        if k % 2 == 0:
            final = pl.ds(size - lanes, lanes)
            product += dot(blocks[slot, rows, final], flipped[slot, final, columns])
        new = keep * factor[k, rows, columns] + add * product
        fresh[k % 2][slot, rows, columns] = new
        value = plus_diagonal(new * shrink[k], i, j, damping * shrink[k])
        b[k, rows, columns] = value.astype(BF16)
        part = jnp.sum(value, axis=0, keepdims=True)
        columns_sum[k][j] = columns_sum[k][j] + part if j in columns_sum[k] else part

    for k in chains:
        for j in offsets:
            for i in offsets:
                gram(k, i, j, pl.ds(i, tile), pl.ds(j, tile))

    def each(step, *targets):
        for k in chains:
            for j in offsets:
                for i in range(0, j + 1, tile):
                    rows, columns = pl.ds(i, tile), pl.ds(j, tile)
                    values = step(k, i, j, rows, columns)
                    for target, value in zip(targets, values):
                        target[k, rows, columns] = value
                        if i != j:
                            target[k, columns, rows] = value.T

    def square(k, i, j, rows, columns):
        return (dot(b[k, rows, :], b[k, :, columns]).astype(BF16),)

    def cube(k, i, j, rows, columns):
        return (dot(b[k, rows, :], u[k, :, columns]).astype(BF16),)

    each(square, u)
    each(cube, w)

    vector = {
        k: jnp.concatenate([columns_sum[k][j] for j in sorted(columns_sum[k])], axis=1) for k in chains
    }
    length = {}
    for matrix in (w, w, b):
        for k in chains:
            vector[k] = vector[k] * lax.rsqrt(jnp.sum(vector[k] * vector[k], axis=1, keepdims=True))
        for k in chains:
            high = vector[k].astype(BF16)
            low = (vector[k] - high.astype(F32)).astype(BF16)
            both = dot(jnp.concatenate([high, low], axis=0), matrix[k])
            vector[k] = both[0:1] + both[1:2]
    for k in chains:
        length[k] = jnp.sqrt(jnp.sum(vector[k] * vector[k], axis=1, keepdims=True))
    c1 = {k: 1.0 / (1.25 * length[k]) for k in chains}
    c2 = {k: c1[k] * c1[k] for k in chains}
    c3 = {k: c2[k] * c1[k] for k in chains}
    scale = {k: lax.rsqrt(jnp.sqrt((1.25 * length[k]) * tops[k])) for k in chains}

    def thin(scalar):
        return scalar.astype(BF16)

    for k in chains:
        v[k] = thin(A4 * c1[k]) * b[k] + thin(A5 * c2[k]) * u[k]

    def second(k, i, j, rows, columns):
        value = c3[k] * dot(w[k, rows, :], v[k, :, columns])
        small = thin(A2 * c2[k]) * u[k, rows, columns] + thin(A3 * c3[k]) * w[k, rows, columns]
        value += (A1 * c1[k]) * b[k, rows, columns].astype(F32) + small.astype(F32)
        return (value.astype(BF16),)

    def square_again(k, i, j, rows, columns):
        return (dot(m[k, rows, :], m[k, :, columns]).astype(BF16),)

    def cube_again(k, i, j, rows, columns):
        product = dot(m[k, rows, :], u[k, :, columns]).astype(BF16)
        mixed = BF16(R4) * m[k, rows, columns] + BF16(R5) * u[k, rows, columns] + BF16(R6) * product
        return (product, mixed)

    def tail(k, i, j, rows, columns):
        small = BF16(R2) * u[k, rows, columns] + BF16(R3) * w[k, rows, columns]
        value = dot(w[k, rows, :], v[k, :, columns]) + small.astype(F32)
        return ((value + R1 * m[k, rows, columns].astype(F32)).astype(BF16),)

    def root(k, i, j, rows, columns):
        value = (1.25 * scale[k]) * m[k, rows, columns].astype(F32)
        value -= (0.25 * R0 * scale[k] * c1[k]) * b[k, rows, columns].astype(F32)
        value -= (0.25 * scale[k] * c1[k]) * dot(b[k, rows, :], m[k, :, columns])
        return (plus_diagonal(value, i, j, (1.25 * R0) * scale[k]).astype(BF16),)

    each(second, m)
    each(square_again, u)
    each(cube_again, w, v)
    each(tail, m)
    each(root, v)

    one, two = chains
    for j in offsets:
        columns = pl.ds(j, tile)
        u[one, :, columns] = dot(v[one], blocks[slot, :, columns]).astype(BF16)
    energy = jnp.zeros((1, 1), F32)
    for j in offsets:
        columns = pl.ds(j, tile)
        shaped = dot(u[one], v[two, :, columns])
        wide[:, columns] = shaped
        energy += whole_sum(shaped * shaped)
    graft = jnp.sqrt(energy_in / (size * size)) / jnp.sqrt(energy / (size * size) + epsilon)
    result[slot] = (wide[...] * graft).astype(BF16)


def step_kernel(
    n_dp, count, lanes, tile, owner_table, grads, left, right, update, left_new, right_new, owners_v, owners_s,
    place_v, place_s, block_v, block_s, stage, raw, raw_in, cross, cross_in, both, both_in, summed, outgoing,
    blocks, flipped, sums, factor, b, u, v, w, m, wide, ready, back, load_sem, factor_sem, table_sem, x_send, x_recv,
    o_send, o_recv, r_send, r_recv,
):
    row, me = lax.axis_index("dp"), lax.axis_index("block")
    stripe = grads.shape[3]
    half = count // 2
    size = grads.shape[4]
    chunks = size // lanes
    near, behind, far = lax.rem(row + 1, n_dp), lax.rem(row + n_dp - 1, n_dp), lax.rem(row + 2, n_dp)

    table_loads = [
        pltpu.make_async_copy(owner_table, owners_v, table_sem.at[0]),
        pltpu.make_async_copy(owner_table, owners_s, table_sem.at[1]),
    ]
    loads = [
        pltpu.make_async_copy(grads.at[0, d], stage.at[n], load_sem.at[n])
        for n, d in enumerate((far, near, behind, row))
    ]
    factor_loads = [
        pltpu.make_async_copy((left, right)[k % 2].at[0, 0, k // 2], factor.at[k], factor_sem.at[k])
        for k in range(2 * MOST)
    ]
    for load in (*loads, *table_loads):
        load.start()

    my_chip, my_core = (me // (2 * SIDE), lax.rem(me // 2, SIDE)), lax.rem(me, 2)

    def partner(hop):
        z, y, core = hop
        chip = lax.rem(my_chip[0] + z, SIDE) * SIDE + lax.rem(my_chip[1] + y, SIDE)
        return chip * 2 + lax.rem(my_core + core, 2)

    barrier = pltpu.get_barrier_semaphore()
    for peer in (near, behind):
        pl.semaphore_signal(barrier, inc=1, device_id=(peer, me), device_id_type=MESH)

    for hop in HOPS:
        pl.semaphore_signal(barrier, inc=1, device_id=(row, partner(hop)), device_id_type=MESH)

    own_rows = pl.ds(pl.multiple_of(me * stripe, stripe), stripe)
    halves = (pl.ds(0, half), pl.ds(half, half))
    towards = (near, behind)

    def cut(n, part, c):
        return stage[n, halves[part], :, pl.ds(c * lanes, lanes)]

    def x_copy(kind, way, c, src, dst):
        return pltpu.make_async_remote_copy(
            src_ref=src.at[way, c],
            dst_ref=dst.at[way, c],
            send_sem=x_send.at[kind, way, c],
            recv_sem=x_recv.at[kind, way, c],
            device_id=(towards[way], me),
            device_id_type=MESH,
        )

    raws = [[x_copy(0, way, c, raw, raw_in) for way in range(2)] for c in range(chunks)]
    crosses = [[x_copy(1, way, c, cross, cross_in) for way in range(2)] for c in range(chunks)]
    boths = [[x_copy(2, way, c, both, both_in) for way in range(2)] for c in range(chunks)]

    def dispatch(c):
        columns = pl.ds(c * lanes, lanes)
        for way in range(2):
            crosses[c][way].wait_recv()
            boths[c][way].wait_recv()
        for part in range(2):
            total = cut(3, part, c) + both_in[part, c].astype(F32) + cross_in[1 - part, c].astype(F32)
            summed[c, halves[part]] = total.astype(BF16)

        for hop in HOPS:
            o = partner(hop)
            for s in range(MOST):
                outgoing[c, o, s] = summed[c, block_s[0, o * MOST + s]]
            pltpu.make_async_remote_copy(
                src_ref=outgoing.at[c, o],
                dst_ref=blocks.at[:, own_rows, columns],
                send_sem=o_send.at[c],
                recv_sem=o_recv.at[c],
                device_id=(row, o),
                device_id_type=MESH,
            ).start()
        for s in range(MOST):
            blocks[s, own_rows, columns] = summed[c, block_s[0, me * MOST + s]]

    def start_raw(c):
        for way in range(2):
            raw[way, c] = cut(0, way, c).astype(BF16)
        if c == 0:
            pl.semaphore_wait(barrier, count + 1)
        for way in range(2):
            raws[c][way].start()

    def start_cross(c):
        for way in range(2):
            cross[way, c] = cut(1 + way, 1 - way, c).astype(BF16)
            crosses[c][way].start()

    energies = [[] for _ in range(MOST)]

    def arrive(c, slots_here):
        if slots_here[0] == 0:
            arrived = outgoing.at[c, pl.ds(0, count - 1)]
            pltpu.make_async_copy(arrived, arrived, o_recv.at[c]).wait()
        for slot in slots_here:
            energies[slot].append(absorb(slot, c, lanes, blocks, flipped, sums, c == chunks - 1))

    loads[0].wait()
    start_raw(0)
    loads[1].wait()
    loads[2].wait()
    start_cross(0)
    start_raw(1)

    for load in table_loads:
        load.wait()
    owners = owners_v[pl.ds(row, 1), :]
    order = lax.broadcasted_iota(jnp.int32, owners.shape, 1)

    def count_same(j, ranks):
        same = (owners == owners_s[row, j]) & (order > j)
        return ranks + jnp.where(same, 1, 0)

    places = owners * MOST + lax.fori_loop(0, count, count_same, jnp.zeros_like(owners))
    place_v[...] = places
    place_copy = pltpu.make_async_copy(place_v, place_s, table_sem.at[2])
    place_copy.start()
    place_copy.wait()
    slots = lax.broadcasted_iota(jnp.int32, block_v.shape, 1)

    def fill(j, held):
        return jnp.where(slots == place_s[0, j], j, held)

    block_v[...] = lax.fori_loop(0, count, fill, jnp.zeros_like(slots))
    block_copy = pltpu.make_async_copy(block_v, block_s, table_sem.at[3])
    block_copy.start()
    block_copy.wait()
    loads[3].wait()
    for load in factor_loads:
        load.start()

    for c in range(chunks):
        if c > 0:
            start_cross(c)
            if c + 1 < chunks:
                start_raw(c + 1)
        for way in range(2):
            raws[c][way].wait_recv()
            both[way, c] = (cut(1 + way, way, c) + raw_in[way, c].astype(F32)).astype(BF16)
            boths[c][way].start()
        if c > 0:
            dispatch(c - 1)
        if c > 1:
            arrive(c - 2, range(MOST))
    dispatch(chunks - 1)
    for load in factor_loads:
        load.wait()
    tops = {k: decay_rate * largest_diagonal(factor, k, size) for k in range(2 * MOST)}
    arrive(chunks - 2, range(MOST))

    for slot in range(MOST):
        arrive(chunks - 1, (slot,))
        used = jnp.where(places == me * MOST + slot, F32(1), F32(0))
        active = jnp.max(used, axis=1, keepdims=True) > 0.5
        energy_in = sum(energies[slot])
        precondition(
            slot, active, tile, lanes, energy_in, tops, blocks, flipped, sums, factor, (left_new, right_new),
            b, u, v, w, m, wide, ready,
        )

        for hop in HOPS:
            o = partner(hop)
            pltpu.make_async_remote_copy(
                src_ref=ready.at[slot, pl.ds(pl.multiple_of(o * stripe, stripe), stripe)],
                dst_ref=back.at[me * MOST + slot],
                send_sem=r_send.at[slot],
                recv_sem=r_recv.at[slot],
                device_id=(row, o),
                device_id_type=MESH,
            ).start()
        back[me * MOST + slot] = ready[slot, own_rows]

    for c in range(chunks):
        for way in range(2):
            raws[c][way].wait_send()
            crosses[c][way].wait_send()
            boths[c][way].wait_send()
        arrived = outgoing.at[c, pl.ds(0, count - 1)]
        pltpu.make_async_copy(arrived, arrived, o_send.at[c]).wait()
    for slot in range(MOST):
        arrived = back.at[pl.ds(0, count - 1)]
        pltpu.make_async_copy(arrived, arrived, r_recv.at[slot]).wait()
        pltpu.make_async_copy(arrived, arrived, r_send.at[slot]).wait()

    def put(j, carry):
        update[j] = back[place_s[0, j]]
        return carry

    lax.fori_loop(0, count, put, 0)


def whole_step(owner_table, grads, left, right, n_dp, lanes, tile):
    _, _, count, stripe, size = grads.shape
    chunks = size // lanes
    part = pltpu.VMEM((2, chunks, count // 2, stripe, lanes), BF16)
    thin = pltpu.VMEM((2 * MOST, size, size), BF16)
    pair = pltpu.VMEM((MOST, size, size), BF16)
    slots = -(-MOST * count // 128) * 128
    DMA = pltpu.SemaphoreType.DMA
    hbm, vmem = pl.BlockSpec(memory_space=pltpu.HBM), pl.BlockSpec(memory_space=pltpu.VMEM)
    return pl.pallas_call(
        functools.partial(step_kernel, n_dp, count, lanes, tile),
        name="shampoo_step",
        out_shape=(
            jax.ShapeDtypeStruct((count, stripe, size), BF16),
            jax.ShapeDtypeStruct((MOST, size, size), F32),
            jax.ShapeDtypeStruct((MOST, size, size), F32),
        ),
        in_specs=[hbm, hbm, hbm, hbm],
        out_specs=(vmem, vmem, vmem),
        scratch_shapes=[
            pltpu.VMEM((n_dp, count), jnp.int32),
            pltpu.SMEM((n_dp, count), jnp.int32),
            pltpu.VMEM((1, count), jnp.int32),
            pltpu.SMEM((1, count), jnp.int32),
            pltpu.VMEM((1, slots), jnp.int32),
            pltpu.SMEM((1, slots), jnp.int32),
            pltpu.VMEM((4, count, stripe, size), F32),
            part, part, part, part, part, part,
            pltpu.VMEM((chunks, count, stripe, lanes), BF16),
            pltpu.VMEM((chunks, count, MOST, stripe, lanes), BF16),
            pair, pair,
            pltpu.VMEM((2 * MOST, size, size), F32),
            pltpu.VMEM((2 * MOST, size, size), F32),
            thin, thin, thin, thin, thin,
            pltpu.VMEM((size, size), F32),
            pair,
            pltpu.VMEM((MOST * count, stripe, size), BF16),
            DMA((4,)), DMA((2 * MOST,)), DMA((4,)), DMA((3, 2, chunks)), DMA((3, 2, chunks)),
            DMA((chunks,)), DMA((chunks,)), DMA((MOST,)), DMA((MOST,)),
        ],
        compiler_params=pltpu.CompilerParams(
            collective_id=0, has_side_effects=True, vmem_limit_bytes=48 * MIB
        ),
    )(owner_table, grads, left, right)


def store_kernel(*refs):
    sources, targets, sems = refs[:3], refs[3:6], refs[6]
    copies = []
    for source, target in zip(sources, targets):
        cuts = PIECES if source.shape[0] % PIECES == 0 else 1
        step = source.shape[0] // cuts
        rows = source.shape[1] // (PIECES // cuts)
        for n in range(PIECES):
            part = (pl.ds(n * step, step),) if cuts > 1 else (slice(None), pl.ds(n * rows, rows))
            copies.append(pltpu.make_async_copy(source.at[part], target.at[part], sems.at[len(copies)]))
    for copy in copies:
        copy.start()
    for copy in copies:
        copy.wait()


def store(*values):
    return pl.pallas_call(
        store_kernel,
        name="store",
        out_shape=tuple(jax.ShapeDtypeStruct(x.shape, x.dtype) for x in values),
        in_specs=[pl.BlockSpec(memory_space=pltpu.VMEM)] * 3,
        out_specs=tuple([pl.BlockSpec(memory_space=pltpu.HBM)] * 3),
        scratch_shapes=[pltpu.SemaphoreType.DMA((3 * PIECES,))],
        compiler_params=pltpu.CompilerParams(vmem_limit_bytes=8 * MIB),
    )(*values)


def local(n_dp, grad_partial, owner_table, left_factor, right_factor):
    values = whole_step(owner_table, grad_partial, left_factor, right_factor, n_dp, 128, 256)
    update, new_left, new_right = store(*values)
    return update[None], new_left[None, None], new_right[None, None]


def solution(mesh):
    return jax.shard_map(
        functools.partial(local, mesh.shape["dp"]),
        mesh=mesh,
        in_specs=(
            P("dp", None, None, "block", None),
            P(),
            P("dp", "block", None, None, None),
            P("dp", "block", None, None, None),
        ),
        out_specs=(
            P("dp", None, "block", None),
            P("dp", "block", None, None, None),
            P("dp", "block", None, None, None),
        ),
        check_vma=False,
    )
```

```python
import functools

import jax
import jax.numpy as jnp
from jax import lax
from jax.experimental import pallas as pl
from jax.experimental.pallas import tpu as pltpu
from jax.sharding import PartitionSpec as P

MOST = 2
POWER = 8
SIDE = 4


def distance(hop):
    return sum(min(steps, SIDE - steps) for steps in hop[:2])


HOPS = sorted(
    ((z, y, core) for z in range(SIDE) for y in range(SIDE) for core in range(2) if (z, y, core) != (0, 0, 0)),
    key=lambda hop: (-distance(hop), (hop[0] + hop[1]) % 2, hop),
)
CHIP_HOPS = [hop for hop in HOPS if hop[2] == 0]
MESH = pl.DeviceIdType.MESH
F32 = jnp.float32
BF16 = jnp.bfloat16
MIB = 1 << 20
PIECES = 4

decay_rate = 0.9
damping = 0.1
epsilon = 1e-06

A1, A2, A3, A4, A5 = 625 / 256, -500 / 256, 150 / 256, -20 / 256, 1 / 256
R0 = 25 / 16
R1 = (-5 - 3125 / 256) / 16
R2 = 3125 / 256 / 16
R3 = -1250 / 256 / 16
R4 = 250 / 256 / 16
R5 = -25 / 256 / 16
R6 = 1 / 256 / 16


def dot(a, b):
    return jnp.dot(a, b, preferred_element_type=F32)


def plus_diagonal(value, i, j, amount):
    tall, broad = value.shape
    if i + tall <= j or j + broad <= i:
        return value
    down = lax.broadcasted_iota(jnp.int32, (tall, broad), 0) + i
    across = lax.broadcasted_iota(jnp.int32, (tall, broad), 1) + j
    return value + jnp.where(down == across, amount, F32(0))


def whole_sum(value):
    return jnp.sum(jnp.sum(value, axis=0, keepdims=True), axis=1, keepdims=True)


def largest_diagonal(factor, k, size):
    best = None
    for i in range(0, size, 128):
        part = factor[k, pl.ds(i, 128), pl.ds(i, 128)]
        down = lax.broadcasted_iota(jnp.int32, (128, 128), 0)
        across = lax.broadcasted_iota(jnp.int32, (128, 128), 1)
        part = jnp.where(down == across, part, F32(0))
        best = part if best is None else jnp.maximum(best, part)
    return jnp.max(jnp.max(best, axis=0, keepdims=True), axis=1, keepdims=True)


def absorb(slot, c, lanes, blocks, flipped, sums, last):
    columns = pl.ds(c * lanes, lanes)
    piece = blocks[slot, :, columns]
    flipped[slot, columns, :] = piece.T
    wide = piece.astype(F32)
    energy = jnp.sum(wide * wide, axis=0, keepdims=True)
    one, two = 2 * slot, 2 * slot + 1
    if not last:
        product = dot(piece, flipped[slot, columns, :])
        sums[one] = product if c == 0 else sums[one] + product
    seen = (c + 1) * lanes
    product = dot(flipped[slot, pl.ds(0, seen), :], piece)
    sums[two, pl.ds(0, seen), columns] = product
    if c > 0:
        sums[two, columns, pl.ds(0, c * lanes)] = product[: c * lanes].T
    return energy


def renew(slot, active, lanes, blocks, flipped, sums, factor, fresh):
    size = blocks.shape[-1]
    keep = jnp.where(active, F32(decay_rate), F32(1.0))
    add = jnp.where(active, F32((1.0 - decay_rate) / size), F32(0.0))
    final = pl.ds(size - lanes, lanes)
    one, two = 2 * slot, 2 * slot + 1
    product = sums[one] + dot(blocks[slot, :, final], flipped[slot, final, :])
    fresh[0][slot] = keep * factor[one] + add * product
    fresh[1][slot] = keep * factor[two] + add * sums[two]


def precondition(slot, tile, lanes, energy_in, tops, blocks, flipped, sums, factor, b, u, v, w, m, wide, result):
    size = blocks.shape[-1]
    chains = (2 * slot, 2 * slot + 1)
    offsets = range(0, size, tile)
    energy_in = jnp.sum(energy_in, axis=1, keepdims=True)
    grown = ((1.0 - decay_rate) / size) * energy_in + damping
    tops = {k: tops[k] + grown for k in chains}
    shrink = {k: 1.0 / tops[k] for k in chains}
    columns_sum = {k: {} for k in chains}

    def gram(k, i, j, rows, columns):
        product = sums[k, rows, columns]
        if k % 2 == 0:
            final = pl.ds(size - lanes, lanes)
            product += dot(blocks[slot, rows, final], flipped[slot, final, columns])
        new = decay_rate * factor[k, rows, columns] + ((1.0 - decay_rate) / size) * product
        value = plus_diagonal(new * shrink[k], i, j, damping * shrink[k])
        b[k, rows, columns] = value.astype(BF16)
        part = jnp.sum(value, axis=0, keepdims=True)
        columns_sum[k][j] = columns_sum[k][j] + part if j in columns_sum[k] else part

    for k in chains:
        for j in offsets:
            for i in offsets:
                gram(k, i, j, pl.ds(i, tile), pl.ds(j, tile))

    def each(step, *targets):
        for k in chains:
            for j in offsets:
                for i in range(0, j + 1, tile):
                    rows, columns = pl.ds(i, tile), pl.ds(j, tile)
                    values = step(k, i, j, rows, columns)
                    for target, value in zip(targets, values):
                        target[k, rows, columns] = value
                        if i != j:
                            target[k, columns, rows] = value.T

    def square(k, i, j, rows, columns):
        return (dot(b[k, rows, :], b[k, :, columns]).astype(BF16),)

    def cube(k, i, j, rows, columns):
        return (dot(b[k, rows, :], u[k, :, columns]).astype(BF16),)

    each(square, u)
    each(cube, w)

    vector = {
        k: jnp.concatenate([columns_sum[k][j] for j in sorted(columns_sum[k])], axis=1) for k in chains
    }
    squares = {}
    for matrix in (w, w, b):
        lines = dict(vector)
        for k in chains:
            high = lines[k].astype(BF16)
            low = (lines[k] - high.astype(F32)).astype(BF16)
            both = dot(jnp.concatenate([high, low], axis=0), matrix[k])
            squares[k] = jnp.sum(lines[k] * lines[k], axis=1, keepdims=True)
            vector[k] = (both[0:1] + both[1:2]) * lax.rsqrt(squares[k])
    length = {k: jnp.sqrt(jnp.sum(vector[k] * vector[k], axis=1, keepdims=True)) for k in chains}
    c1 = {k: 1.0 / (1.25 * length[k]) for k in chains}
    c2 = {k: c1[k] * c1[k] for k in chains}
    c3 = {k: c2[k] * c1[k] for k in chains}
    scale = {k: lax.rsqrt(jnp.sqrt((1.25 * length[k]) * tops[k])) for k in chains}

    def thin(scalar):
        return scalar.astype(BF16)

    for k in chains:
        v[k] = thin(A4 * c1[k]) * b[k] + thin(A5 * c2[k]) * u[k]

    def second(k, i, j, rows, columns):
        value = c3[k] * dot(w[k, rows, :], v[k, :, columns])
        small = thin(A2 * c2[k]) * u[k, rows, columns] + thin(A3 * c3[k]) * w[k, rows, columns]
        value += (A1 * c1[k]) * b[k, rows, columns].astype(F32) + small.astype(F32)
        return (value.astype(BF16),)

    def square_again(k, i, j, rows, columns):
        return (dot(m[k, rows, :], m[k, :, columns]).astype(BF16),)

    def cube_again(k, i, j, rows, columns):
        product = dot(m[k, rows, :], u[k, :, columns]).astype(BF16)
        mixed = BF16(R4) * m[k, rows, columns] + BF16(R5) * u[k, rows, columns] + BF16(R6) * product
        return (product, mixed)

    def tail(k, i, j, rows, columns):
        small = BF16(R2) * u[k, rows, columns] + BF16(R3) * w[k, rows, columns]
        value = dot(w[k, rows, :], v[k, :, columns]) + small.astype(F32)
        return ((value + R1 * m[k, rows, columns].astype(F32)).astype(BF16),)

    def root(k, i, j, rows, columns):
        value = (1.25 * scale[k]) * m[k, rows, columns].astype(F32)
        value -= (0.25 * R0 * scale[k] * c1[k]) * b[k, rows, columns].astype(F32)
        value -= (0.25 * scale[k] * c1[k]) * dot(b[k, rows, :], m[k, :, columns])
        return (plus_diagonal(value, i, j, (1.25 * R0) * scale[k]).astype(BF16),)

    each(second, m)
    each(square_again, u)
    each(cube_again, w, v)
    each(tail, m)
    each(root, v)

    one, two = chains
    for j in offsets:
        columns = pl.ds(j, tile)
        u[one, :, columns] = dot(v[one], blocks[slot, :, columns]).astype(BF16)
    energy = jnp.zeros((1, 1), F32)
    for j in offsets:
        columns = pl.ds(j, tile)
        shaped = dot(u[one], v[two, :, columns])
        wide[:, columns] = shaped
        energy += whole_sum(shaped * shaped)
    graft = jnp.sqrt(energy_in / (size * size)) / jnp.sqrt(energy / (size * size) + epsilon)
    result[slot] = (wide[...] * graft).astype(BF16).reshape(result.shape[1:])


def step_kernel(
    n_dp, count, lanes, tile, owner_table, grads, left, right, update, left_new, right_new, owners_v, owners_s,
    place_v, place_s, block_v, block_s, stage, raw, raw_in, cross, cross_in, both, both_in, summed, outgoing,
    blocks, flipped, sums, factor, b, u, v, w, m, wide, ready, back, load_sem, factor_sem, table_sem, x_send, x_recv,
    o_send, o_recv, r_send, r_recv, hand_sem,
):
    row, me = lax.axis_index("dp"), lax.axis_index("block")
    stripe = grads.shape[3]
    half = count // 2
    size = grads.shape[4]
    chunks = size // lanes
    near, behind, far = lax.rem(row + 1, n_dp), lax.rem(row + n_dp - 1, n_dp), lax.rem(row + 2, n_dp)

    table_loads = [
        pltpu.make_async_copy(owner_table, owners_v, table_sem.at[0]),
        pltpu.make_async_copy(owner_table, owners_s, table_sem.at[1]),
    ]
    loads = [
        pltpu.make_async_copy(grads.at[0, d], stage.at[n], load_sem.at[n])
        for n, d in enumerate((far, near, behind, row))
    ]
    factor_loads = [
        pltpu.make_async_copy((left, right)[k % 2].at[0, 0, k // 2], factor.at[k], factor_sem.at[k])
        for k in range(2 * MOST)
    ]
    for load in (*loads, *table_loads):
        load.start()

    my_chip, my_core = (me // (2 * SIDE), lax.rem(me // 2, SIDE)), lax.rem(me, 2)
    chip = me // 2

    def partner(hop):
        z, y, core = hop
        there = lax.rem(my_chip[0] + z, SIDE) * SIDE + lax.rem(my_chip[1] + y, SIDE)
        return there * 2 + lax.rem(my_core + core, 2)

    barrier = pltpu.get_barrier_semaphore()
    for peer in (near, behind):
        pl.semaphore_signal(barrier, inc=1, device_id=(peer, me), device_id_type=MESH)

    for hop in HOPS:
        pl.semaphore_signal(barrier, inc=1, device_id=(row, partner(hop)), device_id_type=MESH)

    own_rows = pl.ds(pl.multiple_of(me * stripe, stripe), stripe)
    halves = (pl.ds(0, half), pl.ds(half, half))
    towards = (near, behind)

    def cut(n, part, c):
        return stage[n, halves[part], :, pl.ds(c * lanes, lanes)]

    def x_copy(kind, way, c, src, dst):
        return pltpu.make_async_remote_copy(
            src_ref=src.at[way, c],
            dst_ref=dst.at[way, c],
            send_sem=x_send.at[kind, way, c],
            recv_sem=x_recv.at[kind, way, c],
            device_id=(towards[way], me),
            device_id_type=MESH,
        )

    raws = [[x_copy(0, way, c, raw, raw_in) for way in range(2)] for c in range(chunks)]
    crosses = [[x_copy(1, way, c, cross, cross_in) for way in range(2)] for c in range(chunks)]
    boths = [[x_copy(2, way, c, both, both_in) for way in range(2)] for c in range(chunks)]

    def dispatch(c):
        columns = pl.ds(c * lanes, lanes)
        for way in range(2):
            crosses[c][way].wait_recv()
            boths[c][way].wait_recv()
        for part in range(2):
            total = cut(3, part, c) + both_in[part, c].astype(F32) + cross_in[1 - part, c].astype(F32)
            summed[c, halves[part]] = total.astype(BF16)

        for hop in HOPS:
            o = partner(hop)
            for s in range(MOST):
                outgoing[c, o, s] = summed[c, block_s[0, o * MOST + s]]
            pltpu.make_async_remote_copy(
                src_ref=outgoing.at[c, o],
                dst_ref=blocks.at[:, own_rows, columns],
                send_sem=o_send.at[c],
                recv_sem=o_recv.at[c],
                device_id=(row, o),
                device_id_type=MESH,
            ).start()
        for s in range(MOST):
            blocks[s, own_rows, columns] = summed[c, block_s[0, me * MOST + s]]

    def start_raw(c):
        for way in range(2):
            raw[way, c] = cut(0, way, c).astype(BF16)
        if c == 0:
            pl.semaphore_wait(barrier, count + 1)
        for way in range(2):
            raws[c][way].start()

    def start_cross(c):
        for way in range(2):
            cross[way, c] = cut(1 + way, 1 - way, c).astype(BF16)
            crosses[c][way].start()

    energies = [[] for _ in range(MOST)]

    def arrive(c, slots_here):
        if slots_here[0] == 0:
            arrived = outgoing.at[c, pl.ds(0, count - 1)]
            pltpu.make_async_copy(arrived, arrived, o_recv.at[c]).wait()
        for slot in slots_here:
            energies[slot].append(absorb(slot, c, lanes, blocks, flipped, sums, c == chunks - 1))

    loads[0].wait()
    start_raw(0)
    loads[1].wait()
    loads[2].wait()
    start_cross(0)
    start_raw(1)

    for load in table_loads:
        load.wait()
    owners = owners_v[pl.ds(row, 1), :]
    order = lax.broadcasted_iota(jnp.int32, owners.shape, 1)

    def count_same(j, ranks):
        same = (owners == owners_s[row, j]) & (order > j)
        return ranks + jnp.where(same, 1, 0)

    places = owners * MOST + lax.fori_loop(0, count, count_same, jnp.zeros_like(owners))
    place_v[...] = places
    place_copy = pltpu.make_async_copy(place_v, place_s, table_sem.at[2])
    place_copy.start()
    place_copy.wait()
    slots = lax.broadcasted_iota(jnp.int32, block_v.shape, 1)

    def fill(j, held):
        return jnp.where(slots == place_s[0, j], j, held)

    block_v[...] = lax.fori_loop(0, count, fill, jnp.zeros_like(slots))
    block_copy = pltpu.make_async_copy(block_v, block_s, table_sem.at[3])
    block_copy.start()
    block_copy.wait()
    loads[3].wait()
    for load in factor_loads:
        load.start()

    for c in range(chunks):
        if c > 0:
            start_cross(c)
            if c + 1 < chunks:
                start_raw(c + 1)
        for way in range(2):
            raws[c][way].wait_recv()
            both[way, c] = (cut(1 + way, way, c) + raw_in[way, c].astype(F32)).astype(BF16)
            boths[c][way].start()
        if c > 0:
            dispatch(c - 1)
        if c > 1:
            arrive(c - 2, range(MOST))
    dispatch(chunks - 1)
    for load in factor_loads:
        load.wait()
    tops = {k: decay_rate * largest_diagonal(factor, k, size) for k in range(2 * MOST)}
    arrive(chunks - 2, range(MOST))

    for slot in range(MOST):
        arrive(chunks - 1, (slot,))
        energy_in = sum(energies[slot])
        precondition(
            slot, tile, lanes, energy_in, tops, blocks, flipped, sums, factor, b, u, v, w, m, wide, ready
        )

        if slot == 0:
            for hop in CHIP_HOPS:
                o = partner(hop)
                pltpu.make_async_remote_copy(
                    src_ref=ready.at[0, pl.ds(o - my_core, 2)],
                    dst_ref=back.at[pl.ds(0, 2), chip],
                    send_sem=r_send.at[0],
                    recv_sem=r_recv.at[0],
                    device_id=(row, o),
                    device_id_type=MESH,
                ).start()
            for core in range(2):
                back[core, chip] = ready[0, me - my_core + core]
        else:
            for hop in HOPS:
                o = partner(hop)
                pltpu.make_async_remote_copy(
                    src_ref=ready.at[1, o],
                    dst_ref=back.at[3 + my_core, chip],
                    send_sem=r_send.at[1],
                    recv_sem=r_recv.at[1],
                    device_id=(row, o),
                    device_id_type=MESH,
                ).start()
            back[3 + my_core, chip] = ready[1, me]

    chip_pairs = ready.at[0, pl.ds(0, count - 2)]
    pltpu.make_async_copy(chip_pairs, chip_pairs, r_recv.at[0]).wait()
    hand_over = pltpu.make_async_remote_copy(
        src_ref=back.at[1 - my_core],
        dst_ref=back.at[2],
        send_sem=hand_sem.at[0],
        recv_sem=hand_sem.at[1],
        device_id=(row, partner((0, 0, 1))),
        device_id_type=MESH,
    )
    hand_over.start()
    for slot in range(MOST):
        used = jnp.where(places == me * MOST + slot, F32(1), F32(0))
        active = jnp.max(used, axis=1, keepdims=True) > 0.5
        renew(slot, active, lanes, blocks, flipped, sums, factor, (left_new, right_new))

    for c in range(chunks):
        for way in range(2):
            raws[c][way].wait_send()
            crosses[c][way].wait_send()
            boths[c][way].wait_send()
        arrived = outgoing.at[c, pl.ds(0, count - 1)]
        pltpu.make_async_copy(arrived, arrived, o_send.at[c]).wait()
    pltpu.make_async_copy(chip_pairs, chip_pairs, r_send.at[0]).wait()
    hand_over.wait()
    others = ready.at[1, pl.ds(0, count - 1)]
    pltpu.make_async_copy(others, others, r_send.at[1]).wait()
    pltpu.make_async_copy(others, others, r_recv.at[1]).wait()

    def put(j, carry):
        place = place_s[0, j]
        owner, slot = place // MOST, lax.rem(place, MOST)
        owner_chip, owner_core = owner // 2, lax.rem(owner, 2)
        plane = jnp.where(slot == 0, jnp.where(owner_core == my_core, my_core, 2), 3 + owner_core)
        update[j] = back[plane, owner_chip]
        return carry

    lax.fori_loop(0, count, put, 0)


def whole_step(owner_table, grads, left, right, n_dp, lanes, tile):
    _, _, count, stripe, size = grads.shape
    chunks = size // lanes
    part = pltpu.VMEM((2, chunks, count // 2, stripe, lanes), BF16)
    thin = pltpu.VMEM((2 * MOST, size, size), BF16)
    pair = pltpu.VMEM((MOST, size, size), BF16)
    slots = -(-MOST * count // 128) * 128
    DMA = pltpu.SemaphoreType.DMA
    hbm, vmem = pl.BlockSpec(memory_space=pltpu.HBM), pl.BlockSpec(memory_space=pltpu.VMEM)
    return pl.pallas_call(
        functools.partial(step_kernel, n_dp, count, lanes, tile),
        name="shampoo_step",
        out_shape=(
            jax.ShapeDtypeStruct((count, stripe, size), BF16),
            jax.ShapeDtypeStruct((MOST, size, size), F32),
            jax.ShapeDtypeStruct((MOST, size, size), F32),
        ),
        in_specs=[hbm, hbm, hbm, hbm],
        out_specs=(vmem, vmem, vmem),
        scratch_shapes=[
            pltpu.VMEM((n_dp, count), jnp.int32),
            pltpu.SMEM((n_dp, count), jnp.int32),
            pltpu.VMEM((1, count), jnp.int32),
            pltpu.SMEM((1, count), jnp.int32),
            pltpu.VMEM((1, slots), jnp.int32),
            pltpu.SMEM((1, slots), jnp.int32),
            pltpu.VMEM((4, count, stripe, size), F32),
            part, part, part, part, part, part,
            pltpu.VMEM((chunks, count, stripe, lanes), BF16),
            pltpu.VMEM((chunks, count, MOST, stripe, lanes), BF16),
            pair, pair,
            pltpu.VMEM((2 * MOST, size, size), F32),
            pltpu.VMEM((2 * MOST, size, size), F32),
            thin, thin, thin, thin, thin,
            pltpu.VMEM((size, size), F32),
            pltpu.VMEM((MOST, count, stripe, size), BF16),
            pltpu.VMEM((5, count // 2, stripe, size), BF16),
            DMA((4,)), DMA((2 * MOST,)), DMA((4,)), DMA((3, 2, chunks)), DMA((3, 2, chunks)),
            DMA((chunks,)), DMA((chunks,)), DMA((MOST,)), DMA((MOST,)), DMA((2,)),
        ],
        compiler_params=pltpu.CompilerParams(
            collective_id=0, has_side_effects=True, vmem_limit_bytes=48 * MIB
        ),
    )(owner_table, grads, left, right)


def store_kernel(*refs):
    sources, targets, sems = refs[:3], refs[3:6], refs[6]
    copies = []
    for source, target in zip(sources, targets):
        cuts = PIECES if source.shape[0] % PIECES == 0 else 1
        step = source.shape[0] // cuts
        rows = source.shape[1] // (PIECES // cuts)
        for n in range(PIECES):
            part = (pl.ds(n * step, step),) if cuts > 1 else (slice(None), pl.ds(n * rows, rows))
            copies.append(pltpu.make_async_copy(source.at[part], target.at[part], sems.at[len(copies)]))
    for copy in copies:
        copy.start()
    for copy in copies:
        copy.wait()


def store(*values):
    return pl.pallas_call(
        store_kernel,
        name="store",
        out_shape=tuple(jax.ShapeDtypeStruct(x.shape, x.dtype) for x in values),
        in_specs=[pl.BlockSpec(memory_space=pltpu.VMEM)] * 3,
        out_specs=tuple([pl.BlockSpec(memory_space=pltpu.HBM)] * 3),
        scratch_shapes=[pltpu.SemaphoreType.DMA((3 * PIECES,))],
        compiler_params=pltpu.CompilerParams(vmem_limit_bytes=8 * MIB),
    )(*values)


def local(n_dp, grad_partial, owner_table, left_factor, right_factor):
    owner_table = pltpu.with_memory_space_constraint(owner_table, pltpu.HBM)
    values = whole_step(owner_table, grad_partial, left_factor, right_factor, n_dp, 128, 256)
    update, new_left, new_right = store(*values)
    return update[None], new_left[None, None], new_right[None, None]


def solution(mesh):
    return jax.shard_map(
        functools.partial(local, mesh.shape["dp"]),
        mesh=mesh,
        in_specs=(
            P("dp", None, None, "block", None),
            P(),
            P("dp", "block", None, None, None),
            P("dp", "block", None, None, None),
        ),
        out_specs=(
            P("dp", None, "block", None),
            P("dp", "block", None, None, None),
            P("dp", "block", None, None, None),
        ),
        check_vma=False,
    )
```

```python
import functools

import jax
import jax.numpy as jnp
from jax import lax
from jax.experimental import pallas as pl
from jax.experimental.pallas import tpu as pltpu
from jax.sharding import PartitionSpec as P

MOST = 2
POWER = 8
SIDE = 4


def distance(hop):
    return sum(min(steps, SIDE - steps) for steps in hop[:2])


HOPS = sorted(
    ((z, y, core) for z in range(SIDE) for y in range(SIDE) for core in range(2) if (z, y, core) != (0, 0, 0)),
    key=lambda hop: (-distance(hop), (hop[0] + hop[1]) % 2, hop),
)
CHIP_HOPS = [hop for hop in HOPS if hop[2] == 0]
MESH = pl.DeviceIdType.MESH
F32 = jnp.float32
BF16 = jnp.bfloat16
MIB = 1 << 20
PIECES = 4
PER_ROUND = 2

decay_rate = 0.9
damping = 0.1
epsilon = 1e-06

A1, A2, A3, A4, A5 = 625 / 256, -500 / 256, 150 / 256, -20 / 256, 1 / 256
R0 = 25 / 16
R1 = (-5 - 3125 / 256) / 16
R2 = 3125 / 256 / 16
R3 = -1250 / 256 / 16
R4 = 250 / 256 / 16
R5 = -25 / 256 / 16
R6 = 1 / 256 / 16


def dot(a, b):
    return jnp.dot(a, b, preferred_element_type=F32)


def plus_diagonal(value, i, j, amount):
    tall, broad = value.shape
    if i + tall <= j or j + broad <= i:
        return value
    down = lax.broadcasted_iota(jnp.int32, (tall, broad), 0) + i
    across = lax.broadcasted_iota(jnp.int32, (tall, broad), 1) + j
    return value + jnp.where(down == across, amount, F32(0))


def whole_sum(value):
    return jnp.sum(jnp.sum(value, axis=0, keepdims=True), axis=1, keepdims=True)


def largest_diagonal(factor, k, size):
    best = None
    for i in range(0, size, 128):
        part = factor[k, pl.ds(i, 128), pl.ds(i, 128)]
        down = lax.broadcasted_iota(jnp.int32, (128, 128), 0)
        across = lax.broadcasted_iota(jnp.int32, (128, 128), 1)
        part = jnp.where(down == across, part, F32(0))
        best = part if best is None else jnp.maximum(best, part)
    return jnp.max(jnp.max(best, axis=0, keepdims=True), axis=1, keepdims=True)


def absorb(slot, c, lanes, blocks, flipped, sums, last):
    columns = pl.ds(c * lanes, lanes)
    piece = blocks[slot, :, columns]
    flipped[slot, columns, :] = piece.T
    wide = piece.astype(F32)
    energy = jnp.sum(wide * wide, axis=0, keepdims=True)
    one, two = 2 * slot, 2 * slot + 1
    if not last:
        product = dot(piece, flipped[slot, columns, :])
        sums[one] = product if c == 0 else sums[one] + product
    seen = (c + 1) * lanes
    product = dot(flipped[slot, pl.ds(0, seen), :], piece)
    sums[two, pl.ds(0, seen), columns] = product
    if c > 0:
        sums[two, columns, pl.ds(0, c * lanes)] = product[: c * lanes].T
    return energy


def renew(slot, active, lanes, blocks, flipped, sums, factor, fresh):
    size = blocks.shape[-1]
    keep = jnp.where(active, F32(decay_rate), F32(1.0))
    add = jnp.where(active, F32((1.0 - decay_rate) / size), F32(0.0))
    final = pl.ds(size - lanes, lanes)
    one, two = 2 * slot, 2 * slot + 1
    product = sums[one] + dot(blocks[slot, :, final], flipped[slot, final, :])
    fresh[0][slot] = keep * factor[one] + add * product
    fresh[1][slot] = keep * factor[two] + add * sums[two]


def precondition(slot, tile, lanes, energy_in, tops, blocks, flipped, sums, factor, b, u, v, w, m, wide, result):
    size = blocks.shape[-1]
    chains = (2 * slot, 2 * slot + 1)
    offsets = range(0, size, tile)
    energy_in = jnp.sum(energy_in, axis=1, keepdims=True)
    grown = ((1.0 - decay_rate) / size) * energy_in + damping
    tops = {k: tops[k] + grown for k in chains}
    shrink = {k: 1.0 / tops[k] for k in chains}
    columns_sum = {k: {} for k in chains}

    def gram(k, i, j, rows, columns):
        product = sums[k, rows, columns]
        if k % 2 == 0:
            final = pl.ds(size - lanes, lanes)
            product += dot(blocks[slot, rows, final], flipped[slot, final, columns])
        new = decay_rate * factor[k, rows, columns] + ((1.0 - decay_rate) / size) * product
        value = plus_diagonal(new * shrink[k], i, j, damping * shrink[k])
        b[k, rows, columns] = value.astype(BF16)
        part = jnp.sum(value, axis=0, keepdims=True)
        columns_sum[k][j] = columns_sum[k][j] + part if j in columns_sum[k] else part

    for k in chains:
        for j in offsets:
            for i in offsets:
                gram(k, i, j, pl.ds(i, tile), pl.ds(j, tile))

    def each(step, *targets):
        for k in chains:
            for j in offsets:
                for i in range(0, j + 1, tile):
                    rows, columns = pl.ds(i, tile), pl.ds(j, tile)
                    values = step(k, i, j, rows, columns)
                    for target, value in zip(targets, values):
                        target[k, rows, columns] = value
                        if i != j:
                            target[k, columns, rows] = value.T

    def square(k, i, j, rows, columns):
        return (dot(b[k, rows, :], b[k, :, columns]).astype(BF16),)

    def cube(k, i, j, rows, columns):
        return (dot(b[k, rows, :], u[k, :, columns]).astype(BF16),)

    each(square, u)
    each(cube, w)

    vector = {
        k: jnp.concatenate([columns_sum[k][j] for j in sorted(columns_sum[k])], axis=1) for k in chains
    }
    squares = {}
    for matrix in (w, w, b):
        lines = dict(vector)
        for k in chains:
            high = lines[k].astype(BF16)
            low = (lines[k] - high.astype(F32)).astype(BF16)
            both = dot(jnp.concatenate([high, low], axis=0), matrix[k])
            squares[k] = jnp.sum(lines[k] * lines[k], axis=1, keepdims=True)
            vector[k] = (both[0:1] + both[1:2]) * lax.rsqrt(squares[k])
    length = {k: jnp.sqrt(jnp.sum(vector[k] * vector[k], axis=1, keepdims=True)) for k in chains}
    c1 = {k: 1.0 / (1.25 * length[k]) for k in chains}
    c2 = {k: c1[k] * c1[k] for k in chains}
    c3 = {k: c2[k] * c1[k] for k in chains}
    scale = {k: lax.rsqrt(jnp.sqrt((1.25 * length[k]) * tops[k])) for k in chains}

    def thin(scalar):
        return scalar.astype(BF16)

    for k in chains:
        v[k] = thin(A4 * c1[k]) * b[k] + thin(A5 * c2[k]) * u[k]

    def second(k, i, j, rows, columns):
        value = c3[k] * dot(w[k, rows, :], v[k, :, columns])
        small = thin(A2 * c2[k]) * u[k, rows, columns] + thin(A3 * c3[k]) * w[k, rows, columns]
        value += (A1 * c1[k]) * b[k, rows, columns].astype(F32) + small.astype(F32)
        return (value.astype(BF16),)

    def square_again(k, i, j, rows, columns):
        return (dot(m[k, rows, :], m[k, :, columns]).astype(BF16),)

    def cube_again(k, i, j, rows, columns):
        product = dot(m[k, rows, :], u[k, :, columns]).astype(BF16)
        mixed = BF16(R4) * m[k, rows, columns] + BF16(R5) * u[k, rows, columns] + BF16(R6) * product
        return (product, mixed)

    def tail(k, i, j, rows, columns):
        small = BF16(R2) * u[k, rows, columns] + BF16(R3) * w[k, rows, columns]
        value = dot(w[k, rows, :], v[k, :, columns]) + small.astype(F32)
        return ((value + R1 * m[k, rows, columns].astype(F32)).astype(BF16),)

    def root(k, i, j, rows, columns):
        value = (1.25 * scale[k]) * m[k, rows, columns].astype(F32)
        value -= (0.25 * R0 * scale[k] * c1[k]) * b[k, rows, columns].astype(F32)
        value -= (0.25 * scale[k] * c1[k]) * dot(b[k, rows, :], m[k, :, columns])
        return (plus_diagonal(value, i, j, (1.25 * R0) * scale[k]).astype(BF16),)

    each(second, m)
    each(square_again, u)
    each(cube_again, w, v)
    each(tail, m)
    each(root, v)

    one, two = chains
    for j in offsets:
        columns = pl.ds(j, tile)
        u[one, :, columns] = dot(v[one], blocks[slot, :, columns]).astype(BF16)
    energy = jnp.zeros((1, 1), F32)
    for j in offsets:
        columns = pl.ds(j, tile)
        shaped = dot(u[one], v[two, :, columns])
        wide[:, columns] = shaped
        energy += whole_sum(shaped * shaped)
    graft = jnp.sqrt(energy_in / (size * size)) / jnp.sqrt(energy / (size * size) + epsilon)
    result[slot] = (wide[...] * graft).astype(BF16).reshape(result.shape[1:])


def step_kernel(
    n_dp, count, lanes, tile, owner_table, grads, left, right, update, left_new, right_new, owners_v, owners_s,
    place_v, place_s, block_v, block_s, stage, raw, raw_in, cross, cross_in, both, both_in, summed, outgoing,
    blocks, flipped, sums, factor, b, u, v, w, m, wide, ready, back, load_sem, factor_sem, table_sem, x_send, x_recv,
    o_send, o_recv, r_send, r_recv, hand_sem,
):
    row, me = lax.axis_index("dp"), lax.axis_index("block")
    stripe = grads.shape[3]
    half = count // 2
    size = grads.shape[4]
    chunks = size // lanes
    rounds, broad = chunks // PER_ROUND, lanes * PER_ROUND
    near, behind, far = lax.rem(row + 1, n_dp), lax.rem(row + n_dp - 1, n_dp), lax.rem(row + 2, n_dp)

    table_loads = [
        pltpu.make_async_copy(owner_table, owners_v, table_sem.at[0]),
        pltpu.make_async_copy(owner_table, owners_s, table_sem.at[1]),
    ]
    loads = [
        pltpu.make_async_copy(grads.at[0, d], stage.at[n], load_sem.at[n])
        for n, d in enumerate((far, near, behind, row))
    ]
    factor_loads = [
        pltpu.make_async_copy((left, right)[k % 2].at[0, 0, k // 2], factor.at[k], factor_sem.at[k])
        for k in range(2 * MOST)
    ]
    for load in (*loads, *table_loads):
        load.start()

    my_chip, my_core = (me // (2 * SIDE), lax.rem(me // 2, SIDE)), lax.rem(me, 2)
    chip = me // 2

    def partner(hop):
        z, y, core = hop
        there = lax.rem(my_chip[0] + z, SIDE) * SIDE + lax.rem(my_chip[1] + y, SIDE)
        return there * 2 + lax.rem(my_core + core, 2)

    barrier = pltpu.get_barrier_semaphore()
    for peer in (near, behind):
        pl.semaphore_signal(barrier, inc=1, device_id=(peer, me), device_id_type=MESH)

    for hop in HOPS:
        pl.semaphore_signal(barrier, inc=1, device_id=(row, partner(hop)), device_id_type=MESH)

    own_rows = pl.ds(pl.multiple_of(me * stripe, stripe), stripe)
    halves = (pl.ds(0, half), pl.ds(half, half))
    towards = (near, behind)

    def cut(n, part, c):
        return stage[n, halves[part], :, pl.ds(c * lanes, lanes)]

    def x_copy(kind, way, c, src, dst):
        return pltpu.make_async_remote_copy(
            src_ref=src.at[way, c],
            dst_ref=dst.at[way, c],
            send_sem=x_send.at[kind, way, c],
            recv_sem=x_recv.at[kind, way, c],
            device_id=(towards[way], me),
            device_id_type=MESH,
        )

    raws = [[x_copy(0, way, c, raw, raw_in) for way in range(2)] for c in range(chunks)]
    crosses = [[x_copy(1, way, c, cross, cross_in) for way in range(2)] for c in range(chunks)]
    boths = [[x_copy(2, way, c, both, both_in) for way in range(2)] for c in range(chunks)]

    def reduce(c):
        r, columns = c // PER_ROUND, pl.ds((c % PER_ROUND) * lanes, lanes)
        for way in range(2):
            crosses[c][way].wait_recv()
            boths[c][way].wait_recv()
        for part in range(2):
            total = cut(3, part, c) + both_in[part, c].astype(F32) + cross_in[1 - part, c].astype(F32)
            summed[r, halves[part], :, columns] = total.astype(BF16)

    def dispatch(r):
        for o in range(count):
            for s in range(MOST):
                outgoing[r, o, s] = summed[r, block_s[0, o * MOST + s]]
        columns = pl.ds(r * broad, broad)
        for hop in HOPS:
            o = partner(hop)
            pltpu.make_async_remote_copy(
                src_ref=outgoing.at[r, o],
                dst_ref=blocks.at[:, own_rows, columns],
                send_sem=o_send.at[r],
                recv_sem=o_recv.at[r],
                device_id=(row, o),
                device_id_type=MESH,
            ).start()
        blocks[:, own_rows, columns] = outgoing[r, me]

    def start_raw(c):
        for way in range(2):
            raw[way, c] = cut(0, way, c).astype(BF16)
        if c == 0:
            pl.semaphore_wait(barrier, count + 1)
        for way in range(2):
            raws[c][way].start()

    def start_cross(c):
        for way in range(2):
            cross[way, c] = cut(1 + way, 1 - way, c).astype(BF16)
            crosses[c][way].start()

    energies = [[] for _ in range(MOST)]

    def arrive(r):
        arrived = outgoing.at[r, pl.ds(0, count - 1)]
        pltpu.make_async_copy(arrived, arrived, o_recv.at[r]).wait()

    def take(r, slot):
        energies[slot].append(absorb(slot, r, broad, blocks, flipped, sums, r == rounds - 1))

    loads[0].wait()
    start_raw(0)
    loads[1].wait()
    loads[2].wait()
    start_cross(0)
    start_raw(1)
    start_cross(1)

    for load in table_loads:
        load.wait()
    owners = owners_v[pl.ds(row, 1), :]
    order = lax.broadcasted_iota(jnp.int32, owners.shape, 1)

    def count_same(j, ranks):
        same = (owners == owners_s[row, j]) & (order > j)
        return ranks + jnp.where(same, 1, 0)

    places = owners * MOST + lax.fori_loop(0, count, count_same, jnp.zeros_like(owners))
    place_v[...] = places
    place_copy = pltpu.make_async_copy(place_v, place_s, table_sem.at[2])
    place_copy.start()
    place_copy.wait()
    slots = lax.broadcasted_iota(jnp.int32, block_v.shape, 1)

    def fill(j, held):
        return jnp.where(slots == place_s[0, j], j, held)

    block_v[...] = lax.fori_loop(0, count, fill, jnp.zeros_like(slots))
    block_copy = pltpu.make_async_copy(block_v, block_s, table_sem.at[3])
    block_copy.start()
    block_copy.wait()
    loads[3].wait()
    for load in factor_loads:
        load.start()

    for c in range(chunks):
        for way in range(2):
            raws[c][way].wait_recv()
            both[way, c] = (cut(1 + way, way, c) + raw_in[way, c].astype(F32)).astype(BF16)
            boths[c][way].start()
        if c + 2 < chunks:
            start_raw(c + 2)
            start_cross(c + 2)
    for r in range(rounds):
        for c in range(r * PER_ROUND, (r + 1) * PER_ROUND):
            reduce(c)
        dispatch(r)
    for load in factor_loads:
        load.wait()
    tops = {k: decay_rate * largest_diagonal(factor, k, size) for k in range(2 * MOST)}
    for r in range(rounds - 1):
        arrive(r)
        for slot in range(MOST):
            take(r, slot)
    arrive(rounds - 1)

    for slot in range(MOST):
        take(rounds - 1, slot)
        energy_in = sum(energies[slot])
        precondition(
            slot, tile, broad, energy_in, tops, blocks, flipped, sums, factor, b, u, v, w, m, wide, ready
        )

        if slot == 0:
            for hop in CHIP_HOPS:
                o = partner(hop)
                pltpu.make_async_remote_copy(
                    src_ref=ready.at[0, pl.ds(o - my_core, 2)],
                    dst_ref=back.at[pl.ds(0, 2), chip],
                    send_sem=r_send.at[0],
                    recv_sem=r_recv.at[0],
                    device_id=(row, o),
                    device_id_type=MESH,
                ).start()
            for core in range(2):
                back[core, chip] = ready[0, me - my_core + core]
        else:
            for hop in HOPS:
                o = partner(hop)
                pltpu.make_async_remote_copy(
                    src_ref=ready.at[1, o],
                    dst_ref=back.at[3 + my_core, chip],
                    send_sem=r_send.at[1],
                    recv_sem=r_recv.at[1],
                    device_id=(row, o),
                    device_id_type=MESH,
                ).start()
            back[3 + my_core, chip] = ready[1, me]

    chip_pairs = ready.at[0, pl.ds(0, count - 2)]
    pltpu.make_async_copy(chip_pairs, chip_pairs, r_recv.at[0]).wait()
    hand_over = pltpu.make_async_remote_copy(
        src_ref=back.at[1 - my_core],
        dst_ref=back.at[2],
        send_sem=hand_sem.at[0],
        recv_sem=hand_sem.at[1],
        device_id=(row, partner((0, 0, 1))),
        device_id_type=MESH,
    )
    hand_over.start()
    for slot in range(MOST):
        used = jnp.where(places == me * MOST + slot, F32(1), F32(0))
        active = jnp.max(used, axis=1, keepdims=True) > 0.5
        renew(slot, active, broad, blocks, flipped, sums, factor, (left_new, right_new))

    for c in range(chunks):
        for way in range(2):
            raws[c][way].wait_send()
            crosses[c][way].wait_send()
            boths[c][way].wait_send()
    for r in range(rounds):
        arrived = outgoing.at[r, pl.ds(0, count - 1)]
        pltpu.make_async_copy(arrived, arrived, o_send.at[r]).wait()
    pltpu.make_async_copy(chip_pairs, chip_pairs, r_send.at[0]).wait()
    hand_over.wait()
    others = ready.at[1, pl.ds(0, count - 1)]
    pltpu.make_async_copy(others, others, r_send.at[1]).wait()
    pltpu.make_async_copy(others, others, r_recv.at[1]).wait()

    for j in range(count):
        place = place_s[0, j]
        owner, slot = place // MOST, lax.rem(place, MOST)
        owner_chip, owner_core = owner // 2, lax.rem(owner, 2)
        plane = jnp.where(slot == 0, jnp.where(owner_core == my_core, my_core, 2), 3 + owner_core)
        update[j] = back[plane, owner_chip]


def whole_step(owner_table, grads, left, right, n_dp, lanes, tile):
    _, _, count, stripe, size = grads.shape
    chunks = size // lanes
    rounds = chunks // PER_ROUND
    part = pltpu.VMEM((2, chunks, count // 2, stripe, lanes), BF16)
    thin = pltpu.VMEM((2 * MOST, size, size), BF16)
    pair = pltpu.VMEM((MOST, size, size), BF16)
    slots = -(-MOST * count // 128) * 128
    DMA = pltpu.SemaphoreType.DMA
    hbm, vmem = pl.BlockSpec(memory_space=pltpu.HBM), pl.BlockSpec(memory_space=pltpu.VMEM)
    return pl.pallas_call(
        functools.partial(step_kernel, n_dp, count, lanes, tile),
        name="shampoo_step",
        out_shape=(
            jax.ShapeDtypeStruct((count, stripe, size), BF16),
            jax.ShapeDtypeStruct((MOST, size, size), F32),
            jax.ShapeDtypeStruct((MOST, size, size), F32),
        ),
        in_specs=[hbm, hbm, hbm, hbm],
        out_specs=(vmem, vmem, vmem),
        scratch_shapes=[
            pltpu.VMEM((n_dp, count), jnp.int32),
            pltpu.SMEM((n_dp, count), jnp.int32),
            pltpu.VMEM((1, count), jnp.int32),
            pltpu.SMEM((1, count), jnp.int32),
            pltpu.VMEM((1, slots), jnp.int32),
            pltpu.SMEM((1, slots), jnp.int32),
            pltpu.VMEM((4, count, stripe, size), F32),
            part, part, part, part, part, part,
            pltpu.VMEM((rounds, count, stripe, PER_ROUND * lanes), BF16),
            pltpu.VMEM((rounds, count, MOST, stripe, PER_ROUND * lanes), BF16),
            pair, pair,
            pltpu.VMEM((2 * MOST, size, size), F32),
            pltpu.VMEM((2 * MOST, size, size), F32),
            thin, thin, thin, thin, thin,
            pltpu.VMEM((size, size), F32),
            pltpu.VMEM((MOST, count, stripe, size), BF16),
            pltpu.VMEM((5, count // 2, stripe, size), BF16),
            DMA((4,)), DMA((2 * MOST,)), DMA((4,)), DMA((3, 2, chunks)), DMA((3, 2, chunks)),
            DMA((rounds,)), DMA((rounds,)), DMA((MOST,)), DMA((MOST,)), DMA((2,)),
        ],
        compiler_params=pltpu.CompilerParams(
            collective_id=0, has_side_effects=True, vmem_limit_bytes=48 * MIB
        ),
    )(owner_table, grads, left, right)


def store_kernel(*refs):
    sources, targets, sems = refs[:3], refs[3:6], refs[6]
    copies = []
    for source, target in zip(sources, targets):
        cuts = PIECES if source.shape[0] % PIECES == 0 else 1
        step = source.shape[0] // cuts
        rows = source.shape[1] // (PIECES // cuts)
        for n in range(PIECES):
            part = (pl.ds(n * step, step),) if cuts > 1 else (slice(None), pl.ds(n * rows, rows))
            copies.append(pltpu.make_async_copy(source.at[part], target.at[part], sems.at[len(copies)]))
    for copy in copies:
        copy.start()
    for copy in copies:
        copy.wait()


def store(*values):
    return pl.pallas_call(
        store_kernel,
        name="store",
        out_shape=tuple(jax.ShapeDtypeStruct(x.shape, x.dtype) for x in values),
        in_specs=[pl.BlockSpec(memory_space=pltpu.VMEM)] * 3,
        out_specs=tuple([pl.BlockSpec(memory_space=pltpu.HBM)] * 3),
        scratch_shapes=[pltpu.SemaphoreType.DMA((3 * PIECES,))],
        compiler_params=pltpu.CompilerParams(vmem_limit_bytes=8 * MIB),
    )(*values)


def local(n_dp, grad_partial, owner_table, left_factor, right_factor):
    owner_table = pltpu.with_memory_space_constraint(owner_table, pltpu.HBM)
    values = whole_step(owner_table, grad_partial, left_factor, right_factor, n_dp, 128, 256)
    update, new_left, new_right = store(*values)
    return update[None], new_left[None, None], new_right[None, None]


def solution(mesh):
    return jax.shard_map(
        functools.partial(local, mesh.shape["dp"]),
        mesh=mesh,
        in_specs=(
            P("dp", None, None, "block", None),
            P(),
            P("dp", "block", None, None, None),
            P("dp", "block", None, None, None),
        ),
        out_specs=(
            P("dp", None, "block", None),
            P("dp", "block", None, None, None),
            P("dp", "block", None, None, None),
        ),
        check_vma=False,
    )
```

```python
import functools

import jax
import jax.numpy as jnp
from jax import lax
from jax.experimental import pallas as pl
from jax.experimental.pallas import tpu as pltpu
from jax.sharding import PartitionSpec as P

MOST = 2
POWER = 8
SIDE = 4


def distance(hop):
    return sum(min(steps, SIDE - steps) for steps in hop[:2])


HOPS = sorted(
    ((z, y, core) for z in range(SIDE) for y in range(SIDE) for core in range(2) if (z, y, core) != (0, 0, 0)),
    key=lambda hop: (-distance(hop), (hop[0] + hop[1]) % 2, hop),
)
CHIP_HOPS = [hop for hop in HOPS if hop[2] == 0]
MESH = pl.DeviceIdType.MESH
F32 = jnp.float32
BF16 = jnp.bfloat16
MIB = 1 << 20
PIECES = 4

decay_rate = 0.9
damping = 0.1
epsilon = 1e-06

A1, A2, A3, A4, A5 = 625 / 256, -500 / 256, 150 / 256, -20 / 256, 1 / 256
R0 = 25 / 16
R1 = (-5 - 3125 / 256) / 16
R2 = 3125 / 256 / 16
R3 = -1250 / 256 / 16
R4 = 250 / 256 / 16
R5 = -25 / 256 / 16
R6 = 1 / 256 / 16


def dot(a, b):
    return jnp.dot(a, b, preferred_element_type=F32)


def plus_diagonal(value, i, j, amount):
    tall, broad = value.shape
    if i + tall <= j or j + broad <= i:
        return value
    down = lax.broadcasted_iota(jnp.int32, (tall, broad), 0) + i
    across = lax.broadcasted_iota(jnp.int32, (tall, broad), 1) + j
    return value + jnp.where(down == across, amount, F32(0))


def whole_sum(value):
    return jnp.sum(jnp.sum(value, axis=0, keepdims=True), axis=1, keepdims=True)


def largest_diagonal(factor, k, size):
    best = None
    for i in range(0, size, 128):
        part = factor[k, pl.ds(i, 128), pl.ds(i, 128)]
        down = lax.broadcasted_iota(jnp.int32, (128, 128), 0)
        across = lax.broadcasted_iota(jnp.int32, (128, 128), 1)
        part = jnp.where(down == across, part, F32(0))
        best = part if best is None else jnp.maximum(best, part)
    return jnp.max(jnp.max(best, axis=0, keepdims=True), axis=1, keepdims=True)


def absorb(slot, c, lanes, blocks, flipped, sums, last):
    columns = pl.ds(c * lanes, lanes)
    piece = blocks[slot, :, columns]
    flipped[slot, columns, :] = piece.T
    wide = piece.astype(F32)
    energy = jnp.sum(wide * wide, axis=0, keepdims=True)
    one, two = 2 * slot, 2 * slot + 1
    if not last:
        product = dot(piece, flipped[slot, columns, :])
        sums[one] = product if c == 0 else sums[one] + product
    seen = (c + 1) * lanes
    product = dot(flipped[slot, pl.ds(0, seen), :], piece)
    sums[two, pl.ds(0, seen), columns] = product
    if c > 0:
        sums[two, columns, pl.ds(0, c * lanes)] = product[: c * lanes].T
    return energy


def renew(slot, active, lanes, blocks, flipped, sums, factor, fresh):
    size = blocks.shape[-1]
    keep = jnp.where(active, F32(decay_rate), F32(1.0))
    add = jnp.where(active, F32((1.0 - decay_rate) / size), F32(0.0))
    final = pl.ds(size - lanes, lanes)
    one, two = 2 * slot, 2 * slot + 1
    product = sums[one] + dot(blocks[slot, :, final], flipped[slot, final, :])
    fresh[0][slot] = keep * factor[one] + add * product
    fresh[1][slot] = keep * factor[two] + add * sums[two]


def precondition(slot, tile, lanes, energy_in, tops, blocks, flipped, sums, factor, b, u, v, w, m, wide, result):
    size = blocks.shape[-1]
    chains = (2 * slot, 2 * slot + 1)
    offsets = range(0, size, tile)
    energy_in = jnp.sum(energy_in, axis=1, keepdims=True)
    grown = ((1.0 - decay_rate) / size) * energy_in + damping
    tops = {k: tops[k] + grown for k in chains}
    shrink = {k: 1.0 / tops[k] for k in chains}
    columns_sum = {k: {} for k in chains}

    def gram(k, i, j, rows, columns):
        product = sums[k, rows, columns]
        if k % 2 == 0:
            final = pl.ds(size - lanes, lanes)
            product += dot(blocks[slot, rows, final], flipped[slot, final, columns])
        new = decay_rate * factor[k, rows, columns] + ((1.0 - decay_rate) / size) * product
        value = plus_diagonal(new * shrink[k], i, j, damping * shrink[k])
        b[k, rows, columns] = value.astype(BF16)

    for k in chains:
        for j in offsets:
            for i in offsets:
                gram(k, i, j, pl.ds(i, tile), pl.ds(j, tile))

    def each(step, *targets):
        for k in chains:
            for j in offsets:
                for i in range(0, j + 1, tile):
                    rows, columns = pl.ds(i, tile), pl.ds(j, tile)
                    values = step(k, i, j, rows, columns)
                    for target, value in zip(targets, values):
                        target[k, rows, columns] = value
                        if i != j:
                            target[k, columns, rows] = value.T

    def square(k, i, j, rows, columns):
        return (dot(b[k, rows, :], b[k, :, columns]).astype(BF16),)

    def count_in(k, j, value):
        part = jnp.sum(value.astype(F32), axis=0, keepdims=True)
        columns_sum[k][j] = columns_sum[k][j] + part if j in columns_sum[k] else part

    def cube(k, i, j, rows, columns):
        value = dot(b[k, rows, :], u[k, :, columns]).astype(BF16)
        count_in(k, j, value)
        if i != j:
            count_in(k, i, value.T)
        return (value,)

    each(square, u)
    each(cube, w)

    vector = {
        k: jnp.concatenate([columns_sum[k][j] for j in sorted(columns_sum[k])], axis=1) for k in chains
    }
    def times(matrix, k, line):
        high = line.astype(BF16)
        low = (line - high.astype(F32)).astype(BF16)
        both = dot(jnp.concatenate([high, low], axis=0), matrix[k])
        return both[0:1] + both[1:2]

    def inner(one, two):
        return jnp.sum(one * two, axis=1, keepdims=True)

    q = {k: times(w, k, vector[k]) * lax.rsqrt(inner(vector[k], vector[k])) for k in chains}
    r = {k: times(u, k, q[k]) for k in chains}
    length = {k: jnp.sqrt(inner(r[k], r[k]) / inner(q[k], r[k])) for k in chains}
    c1 = {k: 1.0 / (1.25 * length[k]) for k in chains}
    c2 = {k: c1[k] * c1[k] for k in chains}
    c3 = {k: c2[k] * c1[k] for k in chains}
    scale = {k: lax.rsqrt(jnp.sqrt((1.25 * length[k]) * tops[k])) for k in chains}

    def thin(scalar):
        return scalar.astype(BF16)

    for k in chains:
        v[k] = thin(A4 * c1[k]) * b[k] + thin(A5 * c2[k]) * u[k]

    def second(k, i, j, rows, columns):
        value = c3[k] * dot(w[k, rows, :], v[k, :, columns])
        small = thin(A2 * c2[k]) * u[k, rows, columns] + thin(A3 * c3[k]) * w[k, rows, columns]
        value += (A1 * c1[k]) * b[k, rows, columns].astype(F32) + small.astype(F32)
        return (value.astype(BF16),)

    def square_again(k, i, j, rows, columns):
        return (dot(m[k, rows, :], m[k, :, columns]).astype(BF16),)

    def cube_again(k, i, j, rows, columns):
        product = dot(m[k, rows, :], u[k, :, columns]).astype(BF16)
        mixed = BF16(R4) * m[k, rows, columns] + BF16(R5) * u[k, rows, columns] + BF16(R6) * product
        return (product, mixed)

    def tail(k, i, j, rows, columns):
        small = BF16(R2) * u[k, rows, columns] + BF16(R3) * w[k, rows, columns]
        value = dot(w[k, rows, :], v[k, :, columns]) + small.astype(F32)
        return ((value + R1 * m[k, rows, columns].astype(F32)).astype(BF16),)

    def root(k, i, j, rows, columns):
        value = (1.25 * scale[k]) * m[k, rows, columns].astype(F32)
        value -= (0.25 * R0 * scale[k] * c1[k]) * b[k, rows, columns].astype(F32)
        value -= (0.25 * scale[k] * c1[k]) * dot(b[k, rows, :], m[k, :, columns])
        return (plus_diagonal(value, i, j, (1.25 * R0) * scale[k]).astype(BF16),)

    each(second, m)
    each(square_again, u)
    each(cube_again, w, v)
    each(tail, m)
    each(root, v)

    one, two = chains
    for j in offsets:
        columns = pl.ds(j, tile)
        u[one, :, columns] = dot(v[one], blocks[slot, :, columns]).astype(BF16)
    energy = jnp.zeros((1, 1), F32)
    for j in offsets:
        columns = pl.ds(j, tile)
        shaped = dot(u[one], v[two, :, columns])
        wide[:, columns] = shaped
        energy += whole_sum(shaped * shaped)
    graft = jnp.sqrt(energy_in / (size * size)) / jnp.sqrt(energy / (size * size) + epsilon)
    result[slot] = (wide[...] * graft).astype(BF16).reshape(result.shape[1:])


def step_kernel(
    n_dp, count, lanes, tile, owner_table, grads, left, right, update, left_new, right_new, owners_v, owners_s,
    place_v, place_s, block_v, block_s, stage, raw, raw_in, cross, cross_in, both, both_in, summed, outgoing,
    blocks, flipped, sums, factor, b, u, v, w, m, wide, ready, back, load_sem, factor_sem, table_sem, x_send, x_recv,
    o_send, o_recv, r_send, r_recv, hand_sem,
):
    row, me = lax.axis_index("dp"), lax.axis_index("block")
    stripe = grads.shape[3]
    half = count // 2
    size = grads.shape[4]
    chunks = size // lanes
    near, behind, far = lax.rem(row + 1, n_dp), lax.rem(row + n_dp - 1, n_dp), lax.rem(row + 2, n_dp)

    table_loads = [
        pltpu.make_async_copy(owner_table, owners_v, table_sem.at[0]),
        pltpu.make_async_copy(owner_table, owners_s, table_sem.at[1]),
    ]
    loads = [
        pltpu.make_async_copy(grads.at[0, d], stage.at[n], load_sem.at[n])
        for n, d in enumerate((far, near, behind, row))
    ]
    factor_loads = [
        pltpu.make_async_copy((left, right)[k % 2].at[0, 0, k // 2], factor.at[k], factor_sem.at[k])
        for k in range(2 * MOST)
    ]
    for load in (*loads, *table_loads):
        load.start()

    my_chip, my_core = (me // (2 * SIDE), lax.rem(me // 2, SIDE)), lax.rem(me, 2)
    chip = me // 2

    def partner(hop):
        z, y, core = hop
        there = lax.rem(my_chip[0] + z, SIDE) * SIDE + lax.rem(my_chip[1] + y, SIDE)
        return there * 2 + lax.rem(my_core + core, 2)

    barrier = pltpu.get_barrier_semaphore()
    for peer in (near, behind):
        pl.semaphore_signal(barrier, inc=1, device_id=(peer, me), device_id_type=MESH)

    for hop in HOPS:
        pl.semaphore_signal(barrier, inc=1, device_id=(row, partner(hop)), device_id_type=MESH)

    own_rows = pl.ds(pl.multiple_of(me * stripe, stripe), stripe)
    halves = (pl.ds(0, half), pl.ds(half, half))
    towards = (near, behind)

    def cut(n, part, c):
        return stage[n, halves[part], :, pl.ds(c * lanes, lanes)]

    def x_copy(kind, way, c, src, dst):
        return pltpu.make_async_remote_copy(
            src_ref=src.at[way, c],
            dst_ref=dst.at[way, c],
            send_sem=x_send.at[kind, way, c],
            recv_sem=x_recv.at[kind, way, c],
            device_id=(towards[way], me),
            device_id_type=MESH,
        )

    raws = [[x_copy(0, way, c, raw, raw_in) for way in range(2)] for c in range(chunks)]
    crosses = [[x_copy(1, way, c, cross, cross_in) for way in range(2)] for c in range(chunks)]
    boths = [[x_copy(2, way, c, both, both_in) for way in range(2)] for c in range(chunks)]

    def dispatch(c):
        columns = pl.ds(c * lanes, lanes)
        for way in range(2):
            crosses[c][way].wait_recv()
            boths[c][way].wait_recv()
        for part in range(2):
            total = cut(3, part, c) + both_in[part, c].astype(F32) + cross_in[1 - part, c].astype(F32)
            summed[c, halves[part]] = total.astype(BF16)

        for hop in HOPS:
            o = partner(hop)
            for s in range(MOST):
                outgoing[c, o, s] = summed[c, block_s[0, o * MOST + s]]
            pltpu.make_async_remote_copy(
                src_ref=outgoing.at[c, o],
                dst_ref=blocks.at[:, own_rows, columns],
                send_sem=o_send.at[c],
                recv_sem=o_recv.at[c],
                device_id=(row, o),
                device_id_type=MESH,
            ).start()
        for s in range(MOST):
            blocks[s, own_rows, columns] = summed[c, block_s[0, me * MOST + s]]

    def start_raw(c):
        for way in range(2):
            raw[way, c] = cut(0, way, c).astype(BF16)
        if c == 0:
            pl.semaphore_wait(barrier, count + 1)
        for way in range(2):
            raws[c][way].start()

    def start_cross(c):
        for way in range(2):
            cross[way, c] = cut(1 + way, 1 - way, c).astype(BF16)
            crosses[c][way].start()

    energies = [[] for _ in range(MOST)]

    def arrive(c, slots_here):
        if slots_here[0] == 0:
            arrived = outgoing.at[c, pl.ds(0, count - 1)]
            pltpu.make_async_copy(arrived, arrived, o_recv.at[c]).wait()
        for slot in slots_here:
            energies[slot].append(absorb(slot, c, lanes, blocks, flipped, sums, c == chunks - 1))

    loads[0].wait()
    start_raw(0)
    loads[1].wait()
    loads[2].wait()
    start_cross(0)
    start_raw(1)

    for load in table_loads:
        load.wait()
    owners = owners_v[pl.ds(row, 1), :]
    order = lax.broadcasted_iota(jnp.int32, owners.shape, 1)

    def count_same(j, ranks):
        same = (owners == owners_s[row, j]) & (order > j)
        return ranks + jnp.where(same, 1, 0)

    places = owners * MOST + lax.fori_loop(0, count, count_same, jnp.zeros_like(owners))
    place_v[...] = places
    place_copy = pltpu.make_async_copy(place_v, place_s, table_sem.at[2])
    place_copy.start()
    place_copy.wait()
    slots = lax.broadcasted_iota(jnp.int32, block_v.shape, 1)

    def fill(j, held):
        return jnp.where(slots == place_s[0, j], j, held)

    block_v[...] = lax.fori_loop(0, count, fill, jnp.zeros_like(slots))
    block_copy = pltpu.make_async_copy(block_v, block_s, table_sem.at[3])
    block_copy.start()
    block_copy.wait()
    loads[3].wait()
    for load in factor_loads:
        load.start()

    for c in range(chunks):
        if c > 0:
            start_cross(c)
            if c + 1 < chunks:
                start_raw(c + 1)
        for way in range(2):
            raws[c][way].wait_recv()
            both[way, c] = (cut(1 + way, way, c) + raw_in[way, c].astype(F32)).astype(BF16)
            boths[c][way].start()
        if c > 0:
            dispatch(c - 1)
        if c > 1:
            arrive(c - 2, range(MOST))
    dispatch(chunks - 1)
    for load in factor_loads:
        load.wait()
    tops = {k: decay_rate * largest_diagonal(factor, k, size) for k in range(2 * MOST)}
    arrive(chunks - 2, range(MOST))

    for slot in range(MOST):
        arrive(chunks - 1, (slot,))
        energy_in = sum(energies[slot])
        precondition(
            slot, tile, lanes, energy_in, tops, blocks, flipped, sums, factor, b, u, v, w, m, wide, ready
        )

        if slot == 0:
            for hop in CHIP_HOPS:
                o = partner(hop)
                pltpu.make_async_remote_copy(
                    src_ref=ready.at[0, pl.ds(o - my_core, 2)],
                    dst_ref=back.at[pl.ds(0, 2), chip],
                    send_sem=r_send.at[0],
                    recv_sem=r_recv.at[0],
                    device_id=(row, o),
                    device_id_type=MESH,
                ).start()
            for core in range(2):
                back[core, chip] = ready[0, me - my_core + core]
        else:
            for hop in HOPS:
                o = partner(hop)
                pltpu.make_async_remote_copy(
                    src_ref=ready.at[1, o],
                    dst_ref=back.at[3 + my_core, chip],
                    send_sem=r_send.at[1],
                    recv_sem=r_recv.at[1],
                    device_id=(row, o),
                    device_id_type=MESH,
                ).start()
            back[3 + my_core, chip] = ready[1, me]

    chip_pairs = ready.at[0, pl.ds(0, count - 2)]
    pltpu.make_async_copy(chip_pairs, chip_pairs, r_recv.at[0]).wait()
    hand_over = pltpu.make_async_remote_copy(
        src_ref=back.at[1 - my_core],
        dst_ref=back.at[2],
        send_sem=hand_sem.at[0],
        recv_sem=hand_sem.at[1],
        device_id=(row, partner((0, 0, 1))),
        device_id_type=MESH,
    )
    hand_over.start()
    for slot in range(MOST):
        used = jnp.where(places == me * MOST + slot, F32(1), F32(0))
        active = jnp.max(used, axis=1, keepdims=True) > 0.5
        renew(slot, active, lanes, blocks, flipped, sums, factor, (left_new, right_new))

    for c in range(chunks):
        for way in range(2):
            raws[c][way].wait_send()
            crosses[c][way].wait_send()
            boths[c][way].wait_send()
        arrived = outgoing.at[c, pl.ds(0, count - 1)]
        pltpu.make_async_copy(arrived, arrived, o_send.at[c]).wait()
    pltpu.make_async_copy(chip_pairs, chip_pairs, r_send.at[0]).wait()
    hand_over.wait()
    others = ready.at[1, pl.ds(0, count - 1)]
    pltpu.make_async_copy(others, others, r_send.at[1]).wait()
    pltpu.make_async_copy(others, others, r_recv.at[1]).wait()

    for j in range(count):
        place = place_s[0, j]
        owner, slot = place // MOST, lax.rem(place, MOST)
        owner_chip, owner_core = owner // 2, lax.rem(owner, 2)
        plane = jnp.where(slot == 0, jnp.where(owner_core == my_core, my_core, 2), 3 + owner_core)
        update[j] = back[plane, owner_chip]


def whole_step(owner_table, grads, left, right, n_dp, lanes, tile):
    _, _, count, stripe, size = grads.shape
    chunks = size // lanes
    part = pltpu.VMEM((2, chunks, count // 2, stripe, lanes), BF16)
    thin = pltpu.VMEM((2 * MOST, size, size), BF16)
    pair = pltpu.VMEM((MOST, size, size), BF16)
    slots = -(-MOST * count // 128) * 128
    DMA = pltpu.SemaphoreType.DMA
    hbm, vmem = pl.BlockSpec(memory_space=pltpu.HBM), pl.BlockSpec(memory_space=pltpu.VMEM)
    return pl.pallas_call(
        functools.partial(step_kernel, n_dp, count, lanes, tile),
        name="shampoo_step",
        out_shape=(
            jax.ShapeDtypeStruct((count, stripe, size), BF16),
            jax.ShapeDtypeStruct((MOST, size, size), F32),
            jax.ShapeDtypeStruct((MOST, size, size), F32),
        ),
        in_specs=[hbm, hbm, hbm, hbm],
        out_specs=(vmem, vmem, vmem),
        scratch_shapes=[
            pltpu.VMEM((n_dp, count), jnp.int32),
            pltpu.SMEM((n_dp, count), jnp.int32),
            pltpu.VMEM((1, count), jnp.int32),
            pltpu.SMEM((1, count), jnp.int32),
            pltpu.VMEM((1, slots), jnp.int32),
            pltpu.SMEM((1, slots), jnp.int32),
            pltpu.VMEM((4, count, stripe, size), F32),
            part, part, part, part, part, part,
            pltpu.VMEM((chunks, count, stripe, lanes), BF16),
            pltpu.VMEM((chunks, count, MOST, stripe, lanes), BF16),
            pair, pair,
            pltpu.VMEM((2 * MOST, size, size), F32),
            pltpu.VMEM((2 * MOST, size, size), F32),
            thin, thin, thin, thin, thin,
            pltpu.VMEM((size, size), F32),
            pltpu.VMEM((MOST, count, stripe, size), BF16),
            pltpu.VMEM((5, count // 2, stripe, size), BF16),
            DMA((4,)), DMA((2 * MOST,)), DMA((4,)), DMA((3, 2, chunks)), DMA((3, 2, chunks)),
            DMA((chunks,)), DMA((chunks,)), DMA((MOST,)), DMA((MOST,)), DMA((2,)),
        ],
        compiler_params=pltpu.CompilerParams(
            collective_id=0, has_side_effects=True, vmem_limit_bytes=48 * MIB
        ),
    )(owner_table, grads, left, right)


def store_kernel(*refs):
    sources, targets, sems = refs[:3], refs[3:6], refs[6]
    copies = []
    for source, target in zip(sources, targets):
        cuts = PIECES if source.shape[0] % PIECES == 0 else 1
        step = source.shape[0] // cuts
        rows = source.shape[1] // (PIECES // cuts)
        for n in range(PIECES):
            part = (pl.ds(n * step, step),) if cuts > 1 else (slice(None), pl.ds(n * rows, rows))
            copies.append(pltpu.make_async_copy(source.at[part], target.at[part], sems.at[len(copies)]))
    for copy in copies:
        copy.start()
    for copy in copies:
        copy.wait()


def store(*values):
    return pl.pallas_call(
        store_kernel,
        name="store",
        out_shape=tuple(jax.ShapeDtypeStruct(x.shape, x.dtype) for x in values),
        in_specs=[pl.BlockSpec(memory_space=pltpu.VMEM)] * 3,
        out_specs=tuple([pl.BlockSpec(memory_space=pltpu.HBM)] * 3),
        scratch_shapes=[pltpu.SemaphoreType.DMA((3 * PIECES,))],
        compiler_params=pltpu.CompilerParams(vmem_limit_bytes=8 * MIB),
    )(*values)


def local(n_dp, grad_partial, owner_table, left_factor, right_factor):
    owner_table = pltpu.with_memory_space_constraint(owner_table, pltpu.HBM)
    values = whole_step(owner_table, grad_partial, left_factor, right_factor, n_dp, 128, 256)
    update, new_left, new_right = store(*values)
    return update[None], new_left[None, None], new_right[None, None]


def solution(mesh):
    return jax.shard_map(
        functools.partial(local, mesh.shape["dp"]),
        mesh=mesh,
        in_specs=(
            P("dp", None, None, "block", None),
            P(),
            P("dp", "block", None, None, None),
            P("dp", "block", None, None, None),
        ),
        out_specs=(
            P("dp", None, "block", None),
            P("dp", "block", None, None, None),
            P("dp", "block", None, None, None),
        ),
        check_vma=False,
    )
```
